512 devices in a mesh: tm: 8 (over y, core), space: 64 (over z, x).
Axes of the slice: x: 4, y: 4, z: 16, core: 2. Of those that a mesh axis runs over, the one named last changes fastest.
Arguments:
- snapshots: bfloat16 [128, 128, 16384], P('tm', None, 'space'), as said below
- frequencies: int32 [16], replicated, may hold values from 1 to 63, as said below
- offsets: int32 [128], P('tm'), may hold values from 0 to 16383
Outputs:
- modes: float32 [16, 2, 128, 16384], P('tm', None, None, 'space')
The draws below stay inside these ranges and needn't reach their ends.
Inputs may be any that keep to these rules, and one draw needn't show every extreme that they name: `frequencies`: the kept frequency indices are distinct and include 1 and 63. `snapshots`: snapshot values of the record.
All inputs are finite; a program needn't handle non-finite values.
Results may differ from the reference program's by a relative error of at most 0.0041.
Values may be sent and summed in bfloat16 or wider, within the bound.
A program may use at most 64 MiB of HBM per device.

```python
import math
import jax
import jax.numpy as jnp
from jax import lax

NB = 128
NFFT = 128
NF = 16
NCELLS = 16384


def draw_snapshots(key, part):
    keys = jax.random.split(key, 3)
    position = jnp.arange(NCELLS, dtype=jnp.float32) / NCELLS
    cell_scale = 0.3 * jnp.exp(math.log(10.0) * position) * jnp.exp(jax.random.uniform(keys[0], (NCELLS,), jnp.float32, math.log(0.7), math.log(1.4)))
    block_scale = jnp.exp(jax.random.uniform(keys[1], (NB,), jnp.float32, math.log(0.3), math.log(3.0)))
    base = jax.random.normal(keys[2], (NB, NFFT, NCELLS), jnp.float32)
    values = base * block_scale[:, None, None] * cell_scale[None, None, :]
    return values.astype(jnp.bfloat16)


def draw_frequencies(key, part):
    first_key = jax.random.fold_in(key, 11)
    second_key = jax.random.fold_in(key, 12)
    middle = jax.random.permutation(first_key, jnp.arange(2, NFFT // 2 - 1, dtype=jnp.int32))[:NF - 2]
    chosen = jnp.concatenate([jnp.array([1, NFFT // 2 - 1], dtype=jnp.int32), middle])
    shuffle_order = jax.random.permutation(second_key, jnp.arange(NF, dtype=jnp.int32))
    return chosen[shuffle_order]


def plant(result, stream_key, low, top_value):
    longest = result.shape.index(max(result.shape))
    spots = []
    for shift in (0, 1):
        where = [jax.random.randint(jax.random.fold_in(stream_key, axis), (), 0, length) for axis, length in enumerate(result.shape)]
        where[longest] = (where[longest] + shift) % result.shape[longest]
        spots.append(tuple(where))
    return result.at[spots[0]].set(low).at[spots[1]].set(top_value)


def setup_inputs(seed: int = 0) -> dict:
    streams_of = jax.random.split(jax.random.key(seed), 4)
    snapshots = draw_snapshots(jax.random.fold_in(streams_of[3], 71), 0)
    frequencies = draw_frequencies(jax.random.fold_in(streams_of[3], 71), 0)
    offsets = plant(jax.random.randint(streams_of[2], (NB,), 0, NFFT * NB), jax.random.fold_in(streams_of[2], 1), 0, (NFFT * NB) - 1).astype(jnp.int32)
    return {"snapshots": snapshots, "frequencies": frequencies, "offsets": offsets}


def make_angle_table(frequencies, length):
    positions = jnp.arange(length, dtype=jnp.int32)
    turn_counts = frequencies[None, :] * positions[:, None] % length
    radians = turn_counts.astype(jnp.float32) * (2.0 * math.pi / length)
    window = 0.5 - 0.5 * jnp.cos(positions.astype(jnp.float32) * (2.0 * math.pi / length))
    cosine_cols = window[:, None] * jnp.cos(radians)
    sine_cols = window[:, None] * jnp.sin(radians)
    return jnp.concatenate([cosine_cols, sine_cols], axis=1).astype(jnp.bfloat16)

def embed_gram(gram_real, gram_imag):
    top_rows = jnp.stack([gram_real, -gram_imag], axis=-1)
    low_rows = jnp.stack([gram_imag, gram_real], axis=-1)
    order = gram_real.shape[0]
    return jnp.stack([top_rows, low_rows], axis=1).reshape(2 * order, 2 * order)

def reference(snapshots, frequencies, offsets):
    angle_table = make_angle_table(frequencies, NFFT)
    table_rows = angle_table.T

    def one_block(block_pair):
        block_data, block_start = block_pair
        projected = jnp.dot(table_rows.astype(jnp.float32), block_data.astype(jnp.float32), preferred_element_type=jnp.float32)
        cos_part = projected[:NF]
        sin_part = projected[NF:]
        turn_counts = frequencies * block_start % NFFT
        phase = turn_counts.astype(jnp.float32) * (2.0 * math.pi / NFFT)
        cos_phase = jnp.cos(phase)[:, None]
        sin_phase = jnp.sin(phase)[:, None]
        real_part = cos_part * cos_phase - sin_part * sin_phase
        imag_part = -(sin_part * cos_phase + cos_part * sin_phase)
        return jnp.stack([real_part, imag_part]).astype(jnp.bfloat16)
    coeffs = lax.map(one_block, (snapshots, offsets))

    def one_freq(slot_index):
        picked = lax.dynamic_index_in_dim(coeffs, slot_index, axis=2, keepdims=False)
        real_rows = picked[:, 0]
        imag_rows = picked[:, 1]
        real_gram = jnp.dot(real_rows.astype(jnp.float32), real_rows.T.astype(jnp.float32), preferred_element_type=jnp.float32) + jnp.dot(imag_rows.astype(jnp.float32), imag_rows.T.astype(jnp.float32), preferred_element_type=jnp.float32)
        cross = jnp.dot(imag_rows.astype(jnp.float32), real_rows.T.astype(jnp.float32), preferred_element_type=jnp.float32)
        imag_gram = cross - cross.T
        embedded = embed_gram(real_gram / NCELLS, imag_gram / NCELLS)
        lower_factor = jnp.linalg.cholesky(embedded)
        stacked_rows = jnp.stack([real_rows, imag_rows], axis=1).reshape(2 * NB, NCELLS).astype(jnp.float32)
        solved = lax.linalg.triangular_solve(lower_factor, stacked_rows, left_side=True, lower=True)
        return jnp.transpose(solved.reshape(NB, 2, NCELLS), (1, 0, 2))
    return lax.map(one_freq, jnp.arange(NF, dtype=jnp.int32))
```

```python
import functools
import math

import jax
import jax.numpy as jnp
from jax import lax
from jax.experimental import pallas as pl
from jax.experimental.pallas import tpu as pltpu
from jax.sharding import PartitionSpec as P

F32 = jnp.float32
BF16 = jnp.bfloat16

MESH = pl.DeviceIdType.MESH


def exchange_kernel(
    nt, nx, nz, snap_ref, table_ref, rot_ref, q_ref, g_ref,
    work, send, part, got_x, part_z, got_z, ring_z,
    a_send, a_recv, x_send, x_recv, z_send, z_recv, y_send, y_recv, w_send, w_recv, own_sem,
):
    nf_all = rot_ref.shape[0] // 2
    blocks, _, cells = snap_ref.shape
    nf = nf_all // nt
    nb = blocks * nt
    me = lax.axis_index("tm")
    spot = lax.axis_index("space")
    my_z = spot // nx
    my_x = spot % nx

    def tm_peer(d):
        return (lax.rem(me + d, nt), spot)

    def x_peer(d):
        return (me, my_z * nx + lax.rem(my_x + d, nx))

    def z_peer(d):
        return (me, lax.rem(my_z + d, nz) * nx + my_x)

    barrier = pltpu.get_barrier_semaphore()
    for d in range(1, nt):
        pl.semaphore_signal(barrier, inc=1, device_id=tm_peer(d), device_id_type=MESH)
    for d in range(1, nx):
        pl.semaphore_signal(barrier, inc=1, device_id=x_peer(d), device_id_type=MESH)
    for d in range(1, nz):
        pl.semaphore_signal(barrier, inc=1, device_id=z_peer(d), device_id_type=MESH)

    table = table_ref[...]
    for b in range(blocks):
        both = jnp.dot(table, snap_ref[b], preferred_element_type=F32)
        cos_part, sin_part = both[:nf_all], both[nf_all:]
        cos_phase = rot_ref[:nf_all, b:b + 1]
        sin_phase = rot_ref[nf_all:, b:b + 1]
        base = b * 2 * nf_all
        real = cos_part * cos_phase - sin_part * sin_phase
        imag = -(sin_part * cos_phase + cos_part * sin_phase)
        for h in range(cells // 128):
            work[h, base:base + nf_all, :] = real[:, h * 128:(h + 1) * 128]
            work[h, base + nf_all:base + 2 * nf_all, :] = imag[:, h * 128:(h + 1) * 128]
    for j in range(nf_all):
        for half in range(2):
            for h in range(cells // 128):
                rows = work[h, pl.ds(half * nf_all + j, blocks, stride=2 * nf_all), :]
                send[j // nf, j % nf, half, :, h * 128:(h + 1) * 128] = rows.astype(BF16)

    pl.semaphore_wait(barrier, nt - 1 + nx - 1 + nz - 1)

    def a_copy(d):
        return pltpu.make_async_remote_copy(
            src_ref=send.at[lax.rem(me + d, nt)],
            dst_ref=q_ref.at[:, :, pl.ds(pl.multiple_of(me * blocks, blocks), blocks), :],
            send_sem=a_send.at[d], recv_sem=a_recv.at[d],
            device_id=tm_peer(d), device_id_type=MESH)

    own = pltpu.make_async_copy(
        send.at[me], q_ref.at[:, :, pl.ds(pl.multiple_of(me * blocks, blocks), blocks), :], own_sem)
    for d in range(1, nt):
        a_copy(d).start()
    own.start()
    own.wait()
    for d in range(1, nt):
        a_copy(d).wait_recv()

    row = lax.broadcasted_iota(jnp.int32, (nb, nb), 0)
    lane = lax.broadcasted_iota(jnp.int32, (nb, nb), 1)
    for f in range(nf):
        rows = q_ref[f].reshape(2 * nb, cells)
        full = lax.dot_general(rows, rows, (((1,), (1,)), ((), ())), preferred_element_type=F32)
        real = full[:nb, :nb] + full[nb:, nb:]
        imag = full[nb:, :nb] - full[:nb, nb:]
        part[f * nb:(f + 1) * nb, :] = jnp.where(row >= lane, real, imag)

    wide = nf * nb // nx
    thin = wide // nz

    def x_copy(d):
        return pltpu.make_async_remote_copy(
            src_ref=part.at[pl.ds(pl.multiple_of(lax.rem(my_x + d, nx) * wide, wide), wide), :],
            dst_ref=got_x.at[d],
            send_sem=x_send.at[d], recv_sem=x_recv.at[d],
            device_id=x_peer(d), device_id_type=MESH)

    for d in range(1, nx):
        x_copy(d).start()
    total = part[pl.ds(pl.multiple_of(my_x * wide, wide), wide), :]
    for d in range(1, nx):
        x_copy(d).wait_recv()
        total = total + got_x[d]
    for c in range(nz):
        part_z[c] = total[c * thin:(c + 1) * thin, :]

    def z_copy(d):
        return pltpu.make_async_remote_copy(
            src_ref=part_z.at[lax.rem(my_z + d, nz)],
            dst_ref=got_z.at[d],
            send_sem=z_send.at[d], recv_sem=z_recv.at[d],
            device_id=z_peer(d), device_id_type=MESH)

    for d in range(1, nz):
        z_copy(d).start()
    small = part_z[my_z]
    for d in range(1, nz):
        z_copy(d).wait_recv()
        small = small + got_z[d]
    ring_z[my_z] = small

    def y_copy(d):
        return pltpu.make_async_remote_copy(
            src_ref=ring_z.at[my_z],
            dst_ref=ring_z.at[my_z],
            send_sem=y_send.at[d], recv_sem=y_recv.at[d],
            device_id=z_peer(d), device_id_type=MESH)

    for d in range(1, nz):
        y_copy(d).start()
    for d in range(1, nz):
        y_copy(d).wait_recv()
    for c in range(nz):
        got_x[0, c * thin:(c + 1) * thin, :] = ring_z[c]
    mine = pl.ds(pl.multiple_of(my_x * wide, wide), wide)
    g_ref[mine, :] = got_x[0]

    def w_copy(d):
        return pltpu.make_async_remote_copy(
            src_ref=got_x.at[0],
            dst_ref=g_ref.at[mine, :],
            send_sem=w_send.at[d], recv_sem=w_recv.at[d],
            device_id=x_peer(d), device_id_type=MESH)

    for d in range(1, nx):
        w_copy(d).start()
    for d in range(1, nx):
        w_copy(d).wait_recv()
    for d in range(1, nt):
        a_copy(d).wait_send()
    for d in range(1, nx):
        x_copy(d).wait_send()
        w_copy(d).wait_send()
    for d in range(1, nz):
        z_copy(d).wait_send()
        y_copy(d).wait_send()


def exchange(snapshots, table, rotation):
    nt = lax.axis_size("tm")
    nx = 4
    nz = lax.axis_size("space") // nx
    blocks, _, cells = snapshots.shape
    nf_all = rotation.shape[0] // 2
    nf, nb = nf_all // nt, blocks * nt
    wide = nf * nb // nx
    thin = wide // nz
    vm = pl.BlockSpec(memory_space=pltpu.VMEM)
    dma = pltpu.SemaphoreType.DMA
    q, g = pl.pallas_call(
        functools.partial(exchange_kernel, nt, nx, nz),
        out_shape=(jax.ShapeDtypeStruct((nf, 2, nb, cells), BF16), jax.ShapeDtypeStruct((nf * nb, nb), F32)),
        in_specs=[vm, vm, vm], out_specs=(vm, vm),
        scratch_shapes=[
            pltpu.VMEM((cells // 128, blocks * 2 * nf_all, 128), F32),
            pltpu.VMEM((nt, nf, 2, blocks, cells), BF16),
            pltpu.VMEM((nf * nb, nb), F32),
            pltpu.VMEM((nx, wide, nb), F32),
            pltpu.VMEM((nz, thin, nb), F32),
            pltpu.VMEM((nz, thin, nb), F32),
            pltpu.VMEM((nz, thin, nb), F32),
            dma((nt,)), dma((nt,)), dma((nx,)), dma((nx,)), dma((nz,)), dma((nz,)),
            dma((nz,)), dma((nz,)), dma((nx,)), dma((nx,)), dma,
        ],
        compiler_params=pltpu.CompilerParams(
            collective_id=0, has_side_effects=True, vmem_limit_bytes=24 << 20),
        name="exchange_gram",
    )(snapshots, table, rotation)
    return q, g.reshape(nf, nb, nb)


def split2(v):
    hi = v.astype(BF16)
    lo = (v - hi.astype(F32)).astype(BF16)
    return hi, lo


def lane_bcast(v, col):
    return jnp.broadcast_to(v[:, col:col + 1], v.shape)


def factor_kernel(scale, block, q_ref, g_ref, out_ref, m_re, m_im, w_ref):
    nf, _, nb, cells = q_ref.shape
    row8 = lax.broadcasted_iota(jnp.int32, (8, nb), 0)
    lane8 = lax.broadcasted_iota(jnp.int32, (8, nb), 1)
    row = lax.broadcasted_iota(jnp.int32, (nb, nb), 0)
    lane = lax.broadcasted_iota(jnp.int32, (nb, nb), 1)
    for f in range(nf):
        packed = g_ref[f] * scale
        flipped = packed.T
        m_re[f] = jnp.where(row >= lane, packed, flipped)
        m_im[f] = jnp.where(row > lane, -flipped, jnp.where(row < lane, packed, 0.0))
    per = block // 8
    for k in range(nb // block):
        r0 = k * block
        R = [
            [[m_re[f, r0 + 8 * v:r0 + 8 * v + 8, :] for v in range(per)],
             [m_im[f, r0 + 8 * v:r0 + 8 * v + 8, :] for v in range(per)]]
            for f in range(nf)
        ]
        dsel = [[jnp.ones((8, nb), F32) for v in range(per)] for f in range(nf)]
        for p in range(block):
            v0, s = p // 8, p % 8
            col = r0 + p
            at_col = lane8 == col
            for f in range(nf):
                re, im = R[f]
                p_re = jnp.broadcast_to(re[v0][s:s + 1, :], (8, nb))
                p_im = jnp.broadcast_to(im[v0][s:s + 1, :], (8, nb))
                d = lane_bcast(p_re, col)
                inv = 1.0 / d
                dsel[f][v0] = jnp.where(row8 == s, d, dsel[f][v0])
                u_re = jnp.where(at_col, inv, p_re * inv)
                u_im = jnp.where(at_col, 0.0, p_im * inv)
                for v in range(v0, per):
                    if v == v0 and s == 7:
                        continue
                    c_re = lane_bcast(re[v], col)
                    c_im = lane_bcast(im[v], col)
                    if v == v0:
                        below = row8 > s
                        c_re = jnp.where(below, c_re, 0.0)
                        c_im = jnp.where(below, c_im, 0.0)
                        zap = at_col & below
                    else:
                        zap = at_col
                    b_re = jnp.where(zap, 0.0, re[v])
                    b_im = jnp.where(zap, 0.0, im[v])
                    re[v] = b_re - (c_re * u_re - c_im * u_im)
                    im[v] = b_im - (c_re * u_im + c_im * u_re)
        for f in range(nf):
            re, im = R[f]
            n_re, n_im = [], []
            for v in range(per):
                mine = row8 + (r0 + 8 * v)
                rs = lax.rsqrt(dsel[f][v])
                cut = (lane8 > mine) & (lane8 < r0 + block)
                n_re.append(jnp.where(cut, 0.0, jnp.where(lane8 == mine, rs, re[v] * rs)))
                n_im.append(jnp.where(cut | (lane8 == mine), 0.0, im[v] * rs))
            a_re = jnp.concatenate(n_re, axis=0)
            a_im = jnp.concatenate(n_im, axis=0)
            keep = lax.broadcasted_iota(jnp.int32, (block, nb), 1) < r0 + block
            w_ref[f, 0, r0:r0 + block, :] = jnp.where(keep, a_re, 0.0)
            w_ref[f, 1, r0:r0 + block, :] = jnp.where(keep, a_im, 0.0)
            if k + 1 < nb // block:
                rest = nb - r0 - block
                left = jnp.concatenate([a_re, a_im], axis=0).T[r0 + block:, :]
                right = jnp.concatenate(
                    [jnp.concatenate([a_re, a_im], axis=1), jnp.concatenate([a_im, -a_re], axis=1)], axis=0)
                lh, ll = split2(left)
                rh, rl = split2(right)
                lcat = jnp.concatenate([lh, lh, ll], axis=1)
                rcat = jnp.concatenate([rh, rl, rh], axis=0)
                upd = jnp.dot(lcat, rcat, preferred_element_type=F32)
                inside = lax.broadcasted_iota(jnp.int32, (rest, nb), 1)
                inside = (inside >= r0) & (inside < r0 + block)
                m_re[f, r0 + block:, :] = jnp.where(inside, 0.0, m_re[f, r0 + block:, :]) - upd[:, :nb]
                m_im[f, r0 + block:, :] = jnp.where(inside, 0.0, m_im[f, r0 + block:, :]) - upd[:, nb:]
    for f in range(nf):
        w_re, w_im = w_ref[f, 0], w_ref[f, 1]
        rh, rl = split2(w_re)
        ih, il = split2(w_im)
        x_re, x_im = q_ref[f, 0], q_ref[f, 1]
        x = jnp.concatenate([x_re, x_im], axis=0)
        a = jnp.concatenate([rh, -ih], axis=1)
        al = jnp.concatenate([rl, -il], axis=1)
        b = jnp.concatenate([ih, rh], axis=1)
        bl = jnp.concatenate([il, rl], axis=1)
        out_ref[f, 0] = jnp.dot(a, x, preferred_element_type=F32) + jnp.dot(al, x, preferred_element_type=F32)
        out_ref[f, 1] = jnp.dot(b, x, preferred_element_type=F32) + jnp.dot(bl, x, preferred_element_type=F32)


def finish(q, g, scale, block=32):
    nf, _, nb, cells = q.shape
    vm = pl.BlockSpec(memory_space=pltpu.VMEM)
    return pl.pallas_call(
        functools.partial(factor_kernel, scale, block),
        out_shape=jax.ShapeDtypeStruct((nf, 2, nb, cells), F32),
        in_specs=[vm, vm], out_specs=vm,
        scratch_shapes=[pltpu.VMEM((nf, nb, nb), F32), pltpu.VMEM((nf, nb, nb), F32), pltpu.VMEM((nf, 2, nb, nb), F32)],
        compiler_params=pltpu.CompilerParams(vmem_limit_bytes=32 << 20),
        name="factor_apply",
    )(q, g)


def make_angle_table(frequencies, length):
    positions = jnp.arange(length, dtype=jnp.int32)
    turn_counts = frequencies[:, None] * positions[None, :] % length
    radians = turn_counts.astype(jnp.float32) * (2.0 * math.pi / length)
    window = 0.5 - 0.5 * jnp.cos(positions.astype(jnp.float32) * (2.0 * math.pi / length))
    cosine_rows = window[None, :] * jnp.cos(radians)
    sine_rows = window[None, :] * jnp.sin(radians)
    return jnp.concatenate([cosine_rows, sine_rows], axis=0).astype(jnp.bfloat16)


def local(snapshots, frequencies, offsets):
    length = snapshots.shape[1]
    table = make_angle_table(frequencies, length)
    turn_counts = frequencies[:, None] * offsets[None, :] % length
    phase = turn_counts.astype(jnp.float32) * (2.0 * math.pi / length)
    rotation = jnp.concatenate([jnp.cos(phase), jnp.sin(phase)], axis=0)
    total_cells = snapshots.shape[2] * lax.axis_size("space")
    q, g = exchange(snapshots, table, rotation)
    return finish(q, g, 1.0 / total_cells)


def solution(mesh):
    placed = (P("tm", None, "space"), P(), P("tm"))
    return jax.shard_map(
        local, mesh=mesh, in_specs=placed, out_specs=P("tm", None, None, "space"), check_vma=False
    )
```

```python
import functools
import math

import jax
import jax.numpy as jnp
from jax import lax
from jax.experimental import pallas as pl
from jax.experimental.pallas import tpu as pltpu
from jax.sharding import PartitionSpec as P

F32 = jnp.float32
BF16 = jnp.bfloat16

MESH = pl.DeviceIdType.MESH
LANES = 128


def cos_sin(turns, length):
    quarter = length // 4
    shifted = turns + quarter // 2
    quadrant = lax.rem(lax.div(shifted, quarter), 4)
    theta = (lax.rem(shifted, quarter) - quarter // 2).astype(F32) * (2.0 * math.pi / length)
    sq = theta * theta
    cos_small = 1.0 + sq * (-0.5 + sq * (1 / 24 + sq * (-1 / 720 + sq * (1 / 40320 - sq / 3628800))))
    sin_small = theta * (1.0 + sq * (-1 / 6 + sq * (1 / 120 + sq * (-1 / 5040 + sq / 362880))))
    swap = (quadrant == 1) | (quadrant == 3)
    cos_sign = jnp.where((quadrant == 1) | (quadrant == 2), -1.0, 1.0)
    sin_sign = jnp.where(quadrant >= 2, -1.0, 1.0)
    return (
        jnp.where(swap, sin_small, cos_small) * cos_sign,
        jnp.where(swap, cos_small, sin_small) * sin_sign,
    )


def exchange_kernel(
    nt, nx, nl, nh, freq_ref, off_ref, snap_hbm, q_ref, g_ref,
    snap, work, send, part, got, half_sum, got_far,
    in_sem, a_send, a_recv, r_send, r_recv, f_send, f_recv, w_send, w_recv, own_sem,
):
    nf_all = freq_ref.shape[0]
    blocks, length, cells = snap.shape
    nf = nf_all // nt
    nb = blocks * nt
    halves = cells // LANES
    group = nx * nl
    me = lax.axis_index("tm")
    spot = lax.axis_index("space")
    my_far = lax.div(spot, group)
    my_near = lax.rem(spot, group)
    my_l = lax.div(my_near, nx)
    my_x = lax.rem(my_near, nx)

    def tm_peer(d):
        return (lax.rem(me + d, nt), spot)

    def near_slot(dl, dx):
        return lax.rem(my_l + dl, nl) * nx + lax.rem(my_x + dx, nx)

    def near_peer(dl, dx):
        return (me, my_far * group + near_slot(dl, dx))

    def far_peer(d):
        return (me, lax.rem(my_far + d, nh) * group + my_near)

    near = [(dl, dx) for dl in range(nl) for dx in range(nx) if dl or dx]

    barrier = pltpu.get_barrier_semaphore()
    for d in range(1, nh):
        pl.semaphore_signal(barrier, inc=1, device_id=far_peer(d), device_id_type=MESH)
    for d in range(1, nt):
        pl.semaphore_signal(barrier, inc=1, device_id=tm_peer(d), device_id_type=MESH)
    for dl, dx in near:
        pl.semaphore_signal(barrier, inc=1, device_id=near_peer(dl, dx), device_id_type=MESH)

    step = blocks // 4
    loads = [
        pltpu.make_async_copy(snap_hbm.at[pl.ds(i * step, step)], snap.at[pl.ds(i * step, step)], in_sem.at[i])
        for i in range(4)
    ]
    for load in loads:
        load.start()

    row = lax.broadcasted_iota(jnp.int32, (nf_all, length), 0)
    position = lax.broadcasted_iota(jnp.int32, (nf_all, length), 1)
    freq = jnp.zeros((nf_all, length), jnp.int32)
    start = jnp.zeros((nf_all, length), jnp.int32)
    for j in range(nf_all):
        freq = jnp.where(row == j, freq_ref[j], freq)
    for b in range(blocks):
        start = jnp.where(position == b, off_ref[b], start)
    window = 0.5 - 0.5 * cos_sin(position, length)[0]
    cosine, sine = cos_sin(lax.rem(freq * position, length), length)
    table = jnp.concatenate([window * cosine, window * sine], axis=0).astype(BF16)
    cos_phase, sin_phase = cos_sin(lax.rem(freq * lax.rem(start, length), length), length)

    for b in range(blocks):
        if b % step == 0:
            loads[b // step].wait()
        both = jnp.dot(table, snap[b], preferred_element_type=F32)
        cos_part, sin_part = both[:nf_all], both[nf_all:]
        cp, sp = cos_phase[:, b:b + 1], sin_phase[:, b:b + 1]
        base = b * 2 * nf_all
        real = cos_part * cp - sin_part * sp
        imag = -(sin_part * cp + cos_part * sp)
        for h in range(halves):
            work[h, base:base + nf_all, :] = real[:, h * LANES:(h + 1) * LANES]
            work[h, base + nf_all:base + 2 * nf_all, :] = imag[:, h * LANES:(h + 1) * LANES]

    mine = pl.ds(pl.multiple_of(me * blocks, blocks), blocks)

    def a_copy(h, d):
        return pltpu.make_async_remote_copy(
            src_ref=send.at[h, lax.rem(me + d, nt)],
            dst_ref=q_ref.at[:, :, mine, pl.ds(h * LANES, LANES)],
            send_sem=a_send.at[h, d], recv_sem=a_recv.at[h, d],
            device_id=tm_peer(d), device_id_type=MESH)

    own = [
        pltpu.make_async_copy(send.at[h, me], q_ref.at[:, :, mine, pl.ds(h * LANES, LANES)], own_sem.at[h])
        for h in range(halves)
    ]
    for h in range(halves):
        for j in range(nf_all):
            for ri in range(2):
                rows = work[h, pl.ds(ri * nf_all + j, blocks, stride=2 * nf_all), :]
                send[h, j // nf, j % nf, ri] = rows.astype(BF16)
        if h == 0:
            pl.semaphore_wait(barrier, nh - 1 + nt - 1 + group - 1)
        for d in range(1, nt):
            a_copy(h, d).start()
        own[h].start()
    for h in range(halves):
        own[h].wait()
        for d in range(1, nt):
            a_copy(h, d).wait_recv()

    grow = lax.broadcasted_iota(jnp.int32, (nb, nb), 0)
    glane = lax.broadcasted_iota(jnp.int32, (nb, nb), 1)
    for f in range(nf):
        rows = q_ref[f].reshape(2 * nb, cells)
        full = lax.dot_general(rows, rows, (((1,), (1,)), ((), ())), preferred_element_type=F32)
        real = full[:nb, :nb] + full[nb:, nb:]
        imag = full[nb:, :nb] - full[:nb, nb:]
        part[f * nb:(f + 1) * nb, :] = jnp.where(grow >= glane, real, imag)

    wide = nf * nb // group

    def chunk(slot):
        return pl.ds(pl.multiple_of(slot * wide, wide), wide)

    def r_copy(dl, dx):
        i = dl * nx + dx
        return pltpu.make_async_remote_copy(
            src_ref=part.at[chunk(near_slot(dl, dx)), :], dst_ref=got.at[i],
            send_sem=r_send.at[i], recv_sem=r_recv.at[i],
            device_id=near_peer(dl, dx), device_id_type=MESH)

    for dl, dx in near:
        r_copy(dl, dx).start()
    total = part[chunk(my_near), :]
    for dl, dx in near:
        r_copy(dl, dx).wait_recv()
        total = total + got[dl * nx + dx]
    got_far[my_far] = total
    half_sum[...] = total

    def f_copy(d):
        return pltpu.make_async_remote_copy(
            src_ref=half_sum, dst_ref=got_far.at[my_far],
            send_sem=f_send.at[d], recv_sem=f_recv.at[d],
            device_id=far_peer(d), device_id_type=MESH)

    for d in range(1, nh):
        f_copy(d).start()
    for d in range(1, nh):
        f_copy(d).wait_recv()
    total = got_far[0]
    for i in range(1, nh):
        total = total + got_far[i]
    g_ref[chunk(my_near), :] = total

    def w_copy(dl, dx):
        i = dl * nx + dx
        return pltpu.make_async_remote_copy(
            src_ref=g_ref.at[chunk(my_near), :], dst_ref=g_ref.at[chunk(my_near), :],
            send_sem=w_send.at[i], recv_sem=w_recv.at[i],
            device_id=near_peer(dl, dx), device_id_type=MESH)

    for dl, dx in near:
        w_copy(dl, dx).start()
    for h in range(halves):
        for d in range(1, nt):
            a_copy(h, d).wait_send()
    for dl, dx in near:
        r_copy(dl, dx).wait_send()
    for d in range(1, nh):
        f_copy(d).wait_send()
    for dl, dx in near:
        w_copy(dl, dx).wait_recv()
    for dl, dx in near:
        w_copy(dl, dx).wait_send()


def exchange(snapshots, frequencies, offsets):
    nt = lax.axis_size("tm")
    nx, nl = 4, 4
    group = nx * nl
    nh = lax.axis_size("space") // group
    blocks, length, cells = snapshots.shape
    nf_all = frequencies.shape[0]
    nf, nb = nf_all // nt, blocks * nt
    wide = nf * nb // group
    halves = cells // LANES
    vm = pl.BlockSpec(memory_space=pltpu.VMEM)
    sm = pl.BlockSpec(memory_space=pltpu.SMEM)
    dma = pltpu.SemaphoreType.DMA
    q, g = pl.pallas_call(
        functools.partial(exchange_kernel, nt, nx, nl, nh),
        out_shape=(jax.ShapeDtypeStruct((nf, 2, nb, cells), BF16), jax.ShapeDtypeStruct((nf * nb, nb), F32)),
        in_specs=[sm, sm, pl.BlockSpec(memory_space=pltpu.HBM)], out_specs=(vm, vm),
        scratch_shapes=[
            pltpu.VMEM((blocks, length, cells), BF16),
            pltpu.VMEM((halves, blocks * 2 * nf_all, LANES), F32),
            pltpu.VMEM((halves, nt, nf, 2, blocks, LANES), BF16),
            pltpu.VMEM((nf * nb, nb), F32),
            pltpu.VMEM((group, wide, nb), F32),
            pltpu.VMEM((wide, nb), F32),
            pltpu.VMEM((nh, wide, nb), F32),
            dma((4,)), dma((halves, nt)), dma((halves, nt)), dma((group,)), dma((group,)),
            dma((nh,)), dma((nh,)), dma((group,)), dma((group,)), dma((halves,)),
        ],
        compiler_params=pltpu.CompilerParams(
            collective_id=0, has_side_effects=True, vmem_limit_bytes=63 << 20),
        name="exchange_gram",
    )(frequencies, offsets, snapshots)
    return q, g.reshape(nf, nb, nb)


def split2(v):
    hi = v.astype(BF16)
    lo = (v - hi.astype(F32)).astype(BF16)
    return hi, lo


def lane_bcast(v, col):
    return jnp.broadcast_to(v[:, col:col + 1], v.shape)


def factor_kernel(scale, block, q_ref, g_ref, out_ref, m_re, m_im, w_ref):
    nf, _, nb, cells = q_ref.shape
    row8 = lax.broadcasted_iota(jnp.int32, (8, nb), 0)
    lane8 = lax.broadcasted_iota(jnp.int32, (8, nb), 1)
    row = lax.broadcasted_iota(jnp.int32, (nb, nb), 0)
    lane = lax.broadcasted_iota(jnp.int32, (nb, nb), 1)
    for f in range(nf):
        packed = g_ref[f] * scale
        flipped = packed.T
        m_re[f] = jnp.where(row >= lane, packed, flipped)
        m_im[f] = jnp.where(row > lane, -flipped, jnp.where(row < lane, packed, 0.0))
    per = block // 8
    for k in range(nb // block):
        r0 = k * block
        R = [
            [[m_re[f, r0 + 8 * v:r0 + 8 * v + 8, :] for v in range(per)],
             [m_im[f, r0 + 8 * v:r0 + 8 * v + 8, :] for v in range(per)]]
            for f in range(nf)
        ]
        dsel = [[jnp.ones((8, nb), F32) for v in range(per)] for f in range(nf)]
        for p in range(block):
            v0, s = p // 8, p % 8
            col = r0 + p
            at_col = lane8 == col
            for f in range(nf):
                re, im = R[f]
                p_re = jnp.broadcast_to(re[v0][s:s + 1, :], (8, nb))
                p_im = jnp.broadcast_to(im[v0][s:s + 1, :], (8, nb))
                d = lane_bcast(p_re, col)
                inv = 1.0 / d
                dsel[f][v0] = jnp.where(row8 == s, d, dsel[f][v0])
                u_re = jnp.where(at_col, inv, p_re * inv)
                u_im = jnp.where(at_col, 0.0, p_im * inv)
                for v in range(v0, per):
                    if v == v0 and s == 7:
                        continue
                    c_re = lane_bcast(re[v], col)
                    c_im = lane_bcast(im[v], col)
                    if v == v0:
                        below = row8 > s
                        c_re = jnp.where(below, c_re, 0.0)
                        c_im = jnp.where(below, c_im, 0.0)
                        zap = at_col & below
                    else:
                        zap = at_col
                    b_re = jnp.where(zap, 0.0, re[v])
                    b_im = jnp.where(zap, 0.0, im[v])
                    re[v] = b_re - (c_re * u_re - c_im * u_im)
                    im[v] = b_im - (c_re * u_im + c_im * u_re)
        for f in range(nf):
            re, im = R[f]
            n_re, n_im = [], []
            for v in range(per):
                mine = row8 + (r0 + 8 * v)
                rs = lax.rsqrt(dsel[f][v])
                cut = (lane8 > mine) & (lane8 < r0 + block)
                n_re.append(jnp.where(cut, 0.0, jnp.where(lane8 == mine, rs, re[v] * rs)))
                n_im.append(jnp.where(cut | (lane8 == mine), 0.0, im[v] * rs))
            a_re = jnp.concatenate(n_re, axis=0)
            a_im = jnp.concatenate(n_im, axis=0)
            keep = lax.broadcasted_iota(jnp.int32, (block, nb), 1) < r0 + block
            w_ref[f, 0, r0:r0 + block, :] = jnp.where(keep, a_re, 0.0)
            w_ref[f, 1, r0:r0 + block, :] = jnp.where(keep, a_im, 0.0)
            if k + 1 < nb // block:
                rest = nb - r0 - block
                left = jnp.concatenate([a_re, a_im], axis=0).T[r0 + block:, :]
                right = jnp.concatenate(
                    [jnp.concatenate([a_re, a_im], axis=1), jnp.concatenate([a_im, -a_re], axis=1)], axis=0)
                lh, ll = split2(left)
                rh, rl = split2(right)
                lcat = jnp.concatenate([lh, lh, ll], axis=1)
                rcat = jnp.concatenate([rh, rl, rh], axis=0)
                upd = jnp.dot(lcat, rcat, preferred_element_type=F32)
                inside = lax.broadcasted_iota(jnp.int32, (rest, nb), 1)
                inside = (inside >= r0) & (inside < r0 + block)
                m_re[f, r0 + block:, :] = jnp.where(inside, 0.0, m_re[f, r0 + block:, :]) - upd[:, :nb]
                m_im[f, r0 + block:, :] = jnp.where(inside, 0.0, m_im[f, r0 + block:, :]) - upd[:, nb:]
    for f in range(nf):
        w_re, w_im = w_ref[f, 0], w_ref[f, 1]
        rh, rl = split2(w_re)
        ih, il = split2(w_im)
        x_re, x_im = q_ref[f, 0], q_ref[f, 1]
        x = jnp.concatenate([x_re, x_im], axis=0)
        a = jnp.concatenate([rh, -ih], axis=1)
        al = jnp.concatenate([rl, -il], axis=1)
        b = jnp.concatenate([ih, rh], axis=1)
        bl = jnp.concatenate([il, rl], axis=1)
        out_ref[f, 0] = jnp.dot(a, x, preferred_element_type=F32) + jnp.dot(al, x, preferred_element_type=F32)
        out_ref[f, 1] = jnp.dot(b, x, preferred_element_type=F32) + jnp.dot(bl, x, preferred_element_type=F32)


def finish(q, g, scale, block=32):
    nf, _, nb, cells = q.shape
    vm = pl.BlockSpec(memory_space=pltpu.VMEM)
    return pl.pallas_call(
        functools.partial(factor_kernel, scale, block),
        out_shape=jax.ShapeDtypeStruct((nf, 2, nb, cells), F32),
        in_specs=[vm, vm], out_specs=vm,
        scratch_shapes=[pltpu.VMEM((nf, nb, nb), F32), pltpu.VMEM((nf, nb, nb), F32), pltpu.VMEM((nf, 2, nb, nb), F32)],
        compiler_params=pltpu.CompilerParams(vmem_limit_bytes=32 << 20),
        name="factor_apply",
    )(q, g)


def local(snapshots, frequencies, offsets):
    total_cells = snapshots.shape[2] * lax.axis_size("space")
    q, g = exchange(snapshots, frequencies, offsets)
    return finish(q, g, 1.0 / total_cells)


def solution(mesh):
    placed = (P("tm", None, "space"), P(), P("tm"))
    return jax.shard_map(
        local, mesh=mesh, in_specs=placed, out_specs=P("tm", None, None, "space"), check_vma=False
    )
```

```python
import functools
import math

import jax
import jax.numpy as jnp
from jax import lax
from jax.experimental import pallas as pl
from jax.experimental.pallas import tpu as pltpu
from jax.sharding import PartitionSpec as P

F32 = jnp.float32
BF16 = jnp.bfloat16

MESH = pl.DeviceIdType.MESH
LANES = 128


def cos_sin(turns, length):
    quarter = length // 4
    shifted = turns + quarter // 2
    quadrant = lax.rem(lax.div(shifted, quarter), 4)
    theta = (lax.rem(shifted, quarter) - quarter // 2).astype(F32) * (2.0 * math.pi / length)
    sq = theta * theta
    cos_small = 1.0 + sq * (-0.5 + sq * (1 / 24 + sq * (-1 / 720 + sq * (1 / 40320 - sq / 3628800))))
    sin_small = theta * (1.0 + sq * (-1 / 6 + sq * (1 / 120 + sq * (-1 / 5040 + sq / 362880))))
    swap = (quadrant == 1) | (quadrant == 3)
    cos_sign = jnp.where((quadrant == 1) | (quadrant == 2), -1.0, 1.0)
    sin_sign = jnp.where(quadrant >= 2, -1.0, 1.0)
    return (
        jnp.where(swap, sin_small, cos_small) * cos_sign,
        jnp.where(swap, cos_small, sin_small) * sin_sign,
    )


def exchange_kernel(
    nt, nx, nl, nh, freq_ref, off_ref, snap_hbm, q_ref, g_ref,
    snap, work, send, part, got, half_sum, got_far,
    in_sem, a_send, a_recv, r_send, r_recv, f_send, f_recv, w_send, w_recv, own_sem,
):
    nf_all = freq_ref.shape[0]
    blocks, length, cells = snap.shape
    nf = nf_all // nt
    nb = blocks * nt
    halves = cells // LANES
    group = nx * nl
    me = lax.axis_index("tm")
    spot = lax.axis_index("space")
    my_far = lax.div(spot, group)
    my_near = lax.rem(spot, group)
    my_l = lax.div(my_near, nx)
    my_x = lax.rem(my_near, nx)

    def tm_peer(d):
        return (lax.rem(me + d, nt), spot)

    def near_slot(dl, dx):
        return lax.rem(my_l + dl, nl) * nx + lax.rem(my_x + dx, nx)

    def near_peer(dl, dx):
        return (me, my_far * group + near_slot(dl, dx))

    def far_peer(d):
        return (me, lax.rem(my_far + d, nh) * group + my_near)

    near = [(dl, dx) for dl in range(nl) for dx in range(nx) if dl or dx]

    barrier = pltpu.get_barrier_semaphore()
    for d in range(1, nh):
        pl.semaphore_signal(barrier, inc=1, device_id=far_peer(d), device_id_type=MESH)
    for d in range(1, nt):
        pl.semaphore_signal(barrier, inc=1, device_id=tm_peer(d), device_id_type=MESH)
    for dl, dx in near:
        pl.semaphore_signal(barrier, inc=1, device_id=near_peer(dl, dx), device_id_type=MESH)

    step = blocks // 4
    loads = [
        pltpu.make_async_copy(snap_hbm.at[pl.ds(i * step, step)], snap.at[pl.ds(i * step, step)], in_sem.at[i])
        for i in range(4)
    ]
    for load in loads:
        load.start()

    row = lax.broadcasted_iota(jnp.int32, (nf_all, length), 0)
    position = lax.broadcasted_iota(jnp.int32, (nf_all, length), 1)
    freq = jnp.zeros((nf_all, length), jnp.int32)
    start = jnp.zeros((nf_all, length), jnp.int32)
    for j in range(nf_all):
        freq = jnp.where(row == j, freq_ref[j], freq)
    for b in range(blocks):
        start = jnp.where(position == b, off_ref[b], start)
    window = 0.5 - 0.5 * cos_sin(position, length)[0]
    cosine, sine = cos_sin(lax.rem(freq * position, length), length)
    table = jnp.concatenate([window * cosine, window * sine], axis=0).astype(BF16)
    cos_phase, sin_phase = cos_sin(lax.rem(freq * lax.rem(start, length), length), length)

    for b in range(blocks):
        if b % step == 0:
            loads[b // step].wait()
        both = jnp.dot(table, snap[b], preferred_element_type=F32)
        cos_part, sin_part = both[:nf_all], both[nf_all:]
        cp, sp = cos_phase[:, b:b + 1], sin_phase[:, b:b + 1]
        base = b * 2 * nf_all
        real = cos_part * cp - sin_part * sp
        imag = -(sin_part * cp + cos_part * sp)
        for h in range(halves):
            work[h, base:base + nf_all, :] = real[:, h * LANES:(h + 1) * LANES]
            work[h, base + nf_all:base + 2 * nf_all, :] = imag[:, h * LANES:(h + 1) * LANES]

    mine = pl.ds(pl.multiple_of(me * blocks, blocks), blocks)

    def a_copy(h, d):
        return pltpu.make_async_remote_copy(
            src_ref=send.at[h, lax.rem(me + d, nt)],
            dst_ref=q_ref.at[:, :, mine, pl.ds(h * LANES, LANES)],
            send_sem=a_send.at[h, d], recv_sem=a_recv.at[h, d],
            device_id=tm_peer(d), device_id_type=MESH)

    own = [
        pltpu.make_async_copy(send.at[h, me], q_ref.at[:, :, mine, pl.ds(h * LANES, LANES)], own_sem.at[h])
        for h in range(halves)
    ]
    for h in range(halves):
        for j in range(nf_all):
            for ri in range(2):
                rows = work[h, pl.ds(ri * nf_all + j, blocks, stride=2 * nf_all), :]
                send[h, j // nf, j % nf, ri] = rows.astype(BF16)
        if h == 0:
            pl.semaphore_wait(barrier, nh - 1 + nt - 1 + group - 1)
        for d in range(1, nt):
            a_copy(h, d).start()
        own[h].start()
    for h in range(halves):
        own[h].wait()
        for d in range(1, nt):
            a_copy(h, d).wait_recv()

    grow = lax.broadcasted_iota(jnp.int32, (nb, nb), 0)
    glane = lax.broadcasted_iota(jnp.int32, (nb, nb), 1)
    for f in range(nf):
        rows = q_ref[f].reshape(2 * nb, cells)
        full = lax.dot_general(rows, rows, (((1,), (1,)), ((), ())), preferred_element_type=F32)
        real = full[:nb, :nb] + full[nb:, nb:]
        imag = full[nb:, :nb] - full[:nb, nb:]
        part[f * nb:(f + 1) * nb, :] = jnp.where(grow >= glane, real, imag)

    wide = nf * nb // group

    def chunk(slot):
        return pl.ds(pl.multiple_of(slot * wide, wide), wide)

    def r_copy(dl, dx):
        i = dl * nx + dx
        return pltpu.make_async_remote_copy(
            src_ref=part.at[chunk(near_slot(dl, dx)), :], dst_ref=got.at[i],
            send_sem=r_send.at[i], recv_sem=r_recv.at[i],
            device_id=near_peer(dl, dx), device_id_type=MESH)

    for dl, dx in near:
        r_copy(dl, dx).start()
    total = part[chunk(my_near), :]
    for dl, dx in near:
        r_copy(dl, dx).wait_recv()
        total = total + got[dl * nx + dx]
    got_far[my_far] = total
    half_sum[...] = total

    def f_copy(d):
        return pltpu.make_async_remote_copy(
            src_ref=half_sum, dst_ref=got_far.at[my_far],
            send_sem=f_send.at[d], recv_sem=f_recv.at[d],
            device_id=far_peer(d), device_id_type=MESH)

    for d in range(1, nh):
        f_copy(d).start()
    for d in range(1, nh):
        f_copy(d).wait_recv()
    total = got_far[0]
    for i in range(1, nh):
        total = total + got_far[i]
    g_ref[chunk(my_near), :] = total

    def w_copy(dl, dx):
        i = dl * nx + dx
        return pltpu.make_async_remote_copy(
            src_ref=g_ref.at[chunk(my_near), :], dst_ref=g_ref.at[chunk(my_near), :],
            send_sem=w_send.at[i], recv_sem=w_recv.at[i],
            device_id=near_peer(dl, dx), device_id_type=MESH)

    for dl, dx in near:
        w_copy(dl, dx).start()
    for h in range(halves):
        for d in range(1, nt):
            a_copy(h, d).wait_send()
    for dl, dx in near:
        r_copy(dl, dx).wait_send()
    for d in range(1, nh):
        f_copy(d).wait_send()
    for dl, dx in near:
        w_copy(dl, dx).wait_recv()
    for dl, dx in near:
        w_copy(dl, dx).wait_send()


def exchange(snapshots, frequencies, offsets):
    nt = lax.axis_size("tm")
    nx, nl = 4, 4
    group = nx * nl
    nh = lax.axis_size("space") // group
    blocks, length, cells = snapshots.shape
    nf_all = frequencies.shape[0]
    nf, nb = nf_all // nt, blocks * nt
    wide = nf * nb // group
    halves = cells // LANES
    vm = pl.BlockSpec(memory_space=pltpu.VMEM)
    sm = pl.BlockSpec(memory_space=pltpu.SMEM)
    dma = pltpu.SemaphoreType.DMA
    q, g = pl.pallas_call(
        functools.partial(exchange_kernel, nt, nx, nl, nh),
        out_shape=(jax.ShapeDtypeStruct((nf, 2, nb, cells), BF16), jax.ShapeDtypeStruct((nf * nb, nb), F32)),
        in_specs=[sm, sm, pl.BlockSpec(memory_space=pltpu.HBM)], out_specs=(vm, vm),
        scratch_shapes=[
            pltpu.VMEM((blocks, length, cells), BF16),
            pltpu.VMEM((halves, blocks * 2 * nf_all, LANES), F32),
            pltpu.VMEM((halves, nt, nf, 2, blocks, LANES), BF16),
            pltpu.VMEM((nf * nb, nb), F32),
            pltpu.VMEM((group, wide, nb), F32),
            pltpu.VMEM((wide, nb), F32),
            pltpu.VMEM((nh, wide, nb), F32),
            dma((4,)), dma((halves, nt)), dma((halves, nt)), dma((group,)), dma((group,)),
            dma((nh,)), dma((nh,)), dma((group,)), dma((group,)), dma((halves,)),
        ],
        compiler_params=pltpu.CompilerParams(
            collective_id=0, has_side_effects=True, vmem_limit_bytes=53 << 20),
        name="exchange_gram",
    )(frequencies, offsets, snapshots)
    return q, g.reshape(nf, nb, nb)


def split2(v):
    hi = v.astype(BF16)
    lo = (v - hi.astype(F32)).astype(BF16)
    return hi, lo


def lane_bcast(v, col):
    return jnp.broadcast_to(v[:, col:col + 1], v.shape)


def row_bcast(v, s):
    return jnp.broadcast_to(v[s:s + 1, :], v.shape)


def factor_kernel(scale, block, q_ref, g_ref, out_ref, m_re, m_im, w_ref):
    nf, _, nb, cells = q_ref.shape
    row8 = lax.broadcasted_iota(jnp.int32, (8, nb), 0)
    lane8 = lax.broadcasted_iota(jnp.int32, (8, nb), 1)
    row = lax.broadcasted_iota(jnp.int32, (nb, nb), 0)
    lane = lax.broadcasted_iota(jnp.int32, (nb, nb), 1)
    for f in range(nf):
        packed = g_ref[f] * scale
        flipped = packed.T
        m_re[f] = jnp.where(row >= lane, packed, flipped)
        m_im[f] = jnp.where(row > lane, -flipped, jnp.where(row < lane, packed, 0.0))
    per = block // 8
    for k in range(nb // block):
        r0 = k * block
        R = [
            [[m_re[f, r0 + 8 * v:r0 + 8 * v + 8, :] for v in range(per)],
             [m_im[f, r0 + 8 * v:r0 + 8 * v + 8, :] for v in range(per)]]
            for f in range(nf)
        ]
        dsel = [[jnp.ones((8, nb), F32) for v in range(per)] for f in range(nf)]
        for v0 in range(per):
            c0 = r0 + 8 * v0
            B = [
                [[[lane_bcast(R[f][ri][v], c0 + c) for c in range(8)] for v in range(v0, per)] for ri in range(2)]
                for f in range(nf)
            ]
            for s in range(8):
                at_col = lane8 == c0 + s
                below = row8 > s
                for f in range(nf):
                    re, im = R[f]
                    b_re, b_im = B[f]
                    d = row_bcast(b_re[0][s], s)
                    ninv = -1.0 / d
                    dsel[f][v0] = jnp.where(row8 == s, d, dsel[f][v0])
                    p_re, p_im = row_bcast(re[v0], s), row_bcast(im[v0], s)
                    h_re = [row_bcast(b_re[0][c], s) if c > s else None for c in range(8)]
                    h_im = [row_bcast(b_im[0][c], s) if c > s else None for c in range(8)]
                    for v in range(v0, per):
                        i = v - v0
                        if i == 0 and s == 7:
                            continue
                        n_re = b_re[i][s] * ninv
                        n_im = b_im[i][s] * ninv
                        if i == 0:
                            n_re = jnp.where(below, n_re, 0.0)
                            n_im = jnp.where(below, n_im, 0.0)
                        for c in range(s + 1, 8):
                            b_re[i][c], b_im[i][c] = (
                                b_re[i][c] + (n_re * h_re[c] - n_im * h_im[c]),
                                b_im[i][c] + (n_re * h_im[c] + n_im * h_re[c]),
                            )
                        re[v], im[v] = (
                            jnp.where(at_col, n_re, re[v] + (n_re * p_re - n_im * p_im)),
                            jnp.where(at_col, n_im, im[v] + (n_re * p_im + n_im * p_re)),
                        )
        for f in range(nf):
            re, im = R[f]
            n_re, n_im = [], []
            for v in range(per):
                mine = row8 + (r0 + 8 * v)
                rs = lax.rsqrt(dsel[f][v])
                cut = (lane8 > mine) & (lane8 < r0 + block)
                n_re.append(jnp.where(cut, 0.0, jnp.where(lane8 == mine, rs, re[v] * rs)))
                n_im.append(jnp.where(cut | (lane8 == mine), 0.0, im[v] * rs))
            a_re = jnp.concatenate(n_re, axis=0)
            a_im = jnp.concatenate(n_im, axis=0)
            keep = lax.broadcasted_iota(jnp.int32, (block, nb), 1) < r0 + block
            w_ref[f, 0, r0:r0 + block, :] = jnp.where(keep, a_re, 0.0)
            w_ref[f, 1, r0:r0 + block, :] = jnp.where(keep, a_im, 0.0)
            if k + 1 < nb // block:
                rest = nb - r0 - block
                rh, rl = split2(a_re)
                ih, il = split2(a_im)
                lcat = jnp.concatenate([rh, ih, rh, ih, rl, il], axis=0)
                rcat = jnp.concatenate(
                    [jnp.concatenate([rh, ih, rl, il, rh, ih], axis=0),
                     jnp.concatenate([ih, -rh, il, -rl, ih, -rh], axis=0)], axis=1)
                upd = lax.dot_general(lcat, rcat, (((0,), (0,)), ((), ())), preferred_element_type=F32)
                upd = upd[r0 + block:, :]
                inside = lax.broadcasted_iota(jnp.int32, (rest, nb), 1)
                inside = (inside >= r0) & (inside < r0 + block)
                m_re[f, r0 + block:, :] = jnp.where(inside, 0.0, m_re[f, r0 + block:, :]) - upd[:, :nb]
                m_im[f, r0 + block:, :] = jnp.where(inside, 0.0, m_im[f, r0 + block:, :]) - upd[:, nb:]
    for f in range(nf):
        w_re, w_im = w_ref[f, 0], w_ref[f, 1]
        rh, rl = split2(w_re)
        ih, il = split2(w_im)
        x_re, x_im = q_ref[f, 0], q_ref[f, 1]
        x = jnp.concatenate([x_re, x_im], axis=0)
        a = jnp.concatenate([rh, -ih], axis=1)
        al = jnp.concatenate([rl, -il], axis=1)
        b = jnp.concatenate([ih, rh], axis=1)
        bl = jnp.concatenate([il, rl], axis=1)
        out_ref[f, 0] = jnp.dot(a, x, preferred_element_type=F32) + jnp.dot(al, x, preferred_element_type=F32)
        out_ref[f, 1] = jnp.dot(b, x, preferred_element_type=F32) + jnp.dot(bl, x, preferred_element_type=F32)


def finish(q, g, scale, block=16):
    nf, _, nb, cells = q.shape
    vm = pl.BlockSpec(memory_space=pltpu.VMEM)
    return pl.pallas_call(
        functools.partial(factor_kernel, scale, block),
        out_shape=jax.ShapeDtypeStruct((nf, 2, nb, cells), F32),
        in_specs=[vm, vm], out_specs=vm,
        scratch_shapes=[pltpu.VMEM((nf, nb, nb), F32), pltpu.VMEM((nf, nb, nb), F32), pltpu.VMEM((nf, 2, nb, nb), F32)],
        compiler_params=pltpu.CompilerParams(vmem_limit_bytes=32 << 20),
        name="factor_apply",
    )(q, g)


def local(snapshots, frequencies, offsets):
    total_cells = snapshots.shape[2] * lax.axis_size("space")
    q, g = exchange(snapshots, frequencies, offsets)
    return finish(q, g, 1.0 / total_cells)


def solution(mesh):
    placed = (P("tm", None, "space"), P(), P("tm"))
    return jax.shard_map(
        local, mesh=mesh, in_specs=placed, out_specs=P("tm", None, None, "space"), check_vma=False
    )
```

```python
import functools
import math

import jax
import jax.numpy as jnp
from jax import lax
from jax.experimental import pallas as pl
from jax.experimental.pallas import tpu as pltpu
from jax.sharding import PartitionSpec as P

F32 = jnp.float32
BF16 = jnp.bfloat16

MESH = pl.DeviceIdType.MESH
LANES = 128


def cos_sin(turns, length):
    quarter = length // 4
    shifted = turns + quarter // 2
    quadrant = lax.rem(lax.div(shifted, quarter), 4)
    theta = (lax.rem(shifted, quarter) - quarter // 2).astype(F32) * (2.0 * math.pi / length)
    sq = theta * theta
    cos_small = 1.0 + sq * (-0.5 + sq * (1 / 24 + sq * (-1 / 720 + sq * (1 / 40320 - sq / 3628800))))
    sin_small = theta * (1.0 + sq * (-1 / 6 + sq * (1 / 120 + sq * (-1 / 5040 + sq / 362880))))
    swap = (quadrant == 1) | (quadrant == 3)
    cos_sign = jnp.where((quadrant == 1) | (quadrant == 2), -1.0, 1.0)
    sin_sign = jnp.where(quadrant >= 2, -1.0, 1.0)
    return (
        jnp.where(swap, sin_small, cos_small) * cos_sign,
        jnp.where(swap, cos_small, sin_small) * sin_sign,
    )


def exchange_kernel(
    nt, nx, nl, nh, freq_hbm, off_hbm, snap_hbm, q_ref, g_ref,
    freq_ref, off_ref, snap, work, send, part, got, half_sum, got_far,
    in_sem, a_send, a_recv, r_send, r_recv, f_send, f_recv, w_send, w_recv, own_sem,
):
    nf_all = freq_ref.shape[0]
    blocks, length, cells = snap.shape
    nf = nf_all // nt
    nb = blocks * nt
    halves = cells // LANES
    group = nx * nl
    me = lax.axis_index("tm")
    spot = lax.axis_index("space")
    my_far = lax.div(spot, group)
    my_near = lax.rem(spot, group)
    my_l = lax.div(my_near, nx)
    my_x = lax.rem(my_near, nx)

    def tm_peer(d):
        return (lax.rem(me + d, nt), spot)

    def near_slot(dl, dx):
        return lax.rem(my_l + dl, nl) * nx + lax.rem(my_x + dx, nx)

    def near_peer(dl, dx):
        return (me, my_far * group + near_slot(dl, dx))

    def far_peer(d):
        return (me, lax.rem(my_far + d, nh) * group + my_near)

    order = (2, 1, 3, 0)
    near = [(dl, dx) for dl in order for dx in order if dl or dx]

    barrier = pltpu.get_barrier_semaphore()
    for d in range(1, nh):
        pl.semaphore_signal(barrier, inc=1, device_id=far_peer(d), device_id_type=MESH)
    for dl, dx in near:
        pl.semaphore_signal(barrier, inc=1, device_id=near_peer(dl, dx), device_id_type=MESH)
    for d in range(1, nt):
        pl.semaphore_signal(barrier, inc=1, device_id=tm_peer(d), device_id_type=MESH)

    small = [
        pltpu.make_async_copy(freq_hbm, freq_ref, in_sem.at[4]),
        pltpu.make_async_copy(off_hbm, off_ref, in_sem.at[5]),
    ]
    for load in small:
        load.start()
    step = blocks // 4
    loads = [
        pltpu.make_async_copy(snap_hbm.at[pl.ds(i * step, step)], snap.at[pl.ds(i * step, step)], in_sem.at[i])
        for i in range(4)
    ]
    for load in loads:
        load.start()

    row = lax.broadcasted_iota(jnp.int32, (nf_all, length), 0)
    position = lax.broadcasted_iota(jnp.int32, (nf_all, length), 1)
    for load in small:
        load.wait()
    freq = jnp.zeros((nf_all, length), jnp.int32)
    start = jnp.zeros((nf_all, length), jnp.int32)
    for j in range(nf_all):
        freq = jnp.where(row == j, freq_ref[j], freq)
    for b in range(blocks):
        start = jnp.where(position == b, off_ref[b], start)
    window = 0.5 - 0.5 * cos_sin(position, length)[0]
    cosine, sine = cos_sin(lax.rem(freq * position, length), length)
    table = jnp.concatenate([window * cosine, window * sine], axis=0).astype(BF16)
    cos_phase, sin_phase = cos_sin(lax.rem(freq * lax.rem(start, length), length), length)

    for b in range(blocks):
        if b % step == 0:
            loads[b // step].wait()
        both = jnp.dot(table, snap[b], preferred_element_type=F32)
        cos_part, sin_part = both[:nf_all], both[nf_all:]
        cp, sp = cos_phase[:, b:b + 1], sin_phase[:, b:b + 1]
        base = b * 2 * nf_all
        real = cos_part * cp - sin_part * sp
        imag = -(sin_part * cp + cos_part * sp)
        for h in range(halves):
            work[h, base:base + nf_all, :] = real[:, h * LANES:(h + 1) * LANES]
            work[h, base + nf_all:base + 2 * nf_all, :] = imag[:, h * LANES:(h + 1) * LANES]

    mine = pl.ds(pl.multiple_of(me * blocks, blocks), blocks)

    def a_copy(f, d):
        return pltpu.make_async_remote_copy(
            src_ref=send.at[f, lax.rem(me + d, nt)],
            dst_ref=q_ref.at[f, :, mine, :],
            send_sem=a_send.at[f, d], recv_sem=a_recv.at[f, d],
            device_id=tm_peer(d), device_id_type=MESH)

    own = [pltpu.make_async_copy(send.at[f, me], q_ref.at[f, :, mine, :], own_sem.at[f]) for f in range(nf)]
    for f in range(nf):
        for t in range(nt):
            for ri in range(2):
                for h in range(halves):
                    rows = work[h, pl.ds(ri * nf_all + t * nf + f, blocks, stride=2 * nf_all), :]
                    send[f, t, ri, :, h * LANES:(h + 1) * LANES] = rows.astype(BF16)
        if f == 0:
            pl.semaphore_wait(barrier, nh - 1 + nt - 1 + group - 1)
        for d in range(1, nt):
            a_copy(f, d).start()
        own[f].start()

    grow = lax.broadcasted_iota(jnp.int32, (nb, nb), 0)
    glane = lax.broadcasted_iota(jnp.int32, (nb, nb), 1)
    wide = nb // group

    def chunk(slot):
        return pl.ds(pl.multiple_of(slot * wide, wide), wide)

    def r_copy(f, dl, dx):
        i = dl * nx + dx
        return pltpu.make_async_remote_copy(
            src_ref=part.at[f, chunk(near_slot(dl, dx)), :], dst_ref=got.at[f, i],
            send_sem=r_send.at[f, i], recv_sem=r_recv.at[f, i],
            device_id=near_peer(dl, dx), device_id_type=MESH)

    def f_copy(f, d):
        return pltpu.make_async_remote_copy(
            src_ref=half_sum.at[f], dst_ref=got_far.at[f, my_far],
            send_sem=f_send.at[f, d], recv_sem=f_recv.at[f, d],
            device_id=far_peer(d), device_id_type=MESH)

    def w_copy(f, dl, dx):
        i = dl * nx + dx
        return pltpu.make_async_remote_copy(
            src_ref=g_ref.at[f, chunk(my_near), :], dst_ref=g_ref.at[f, chunk(my_near), :],
            send_sem=w_send.at[f, i], recv_sem=w_recv.at[f, i],
            device_id=near_peer(dl, dx), device_id_type=MESH)

    for f in range(nf):
        own[f].wait()
        for d in range(1, nt):
            a_copy(f, d).wait_recv()
        rows = q_ref[f].reshape(2 * nb, cells)
        full = lax.dot_general(rows, rows, (((1,), (1,)), ((), ())), preferred_element_type=F32)
        real = full[:nb, :nb] + full[nb:, nb:]
        imag = full[nb:, :nb] - full[:nb, nb:]
        part[f] = jnp.where(grow >= glane, real, imag)
        for dl, dx in near:
            r_copy(f, dl, dx).start()
    for f in range(nf):
        total = part[f, chunk(my_near), :]
        for dl, dx in near:
            r_copy(f, dl, dx).wait_recv()
            total = total + got[f, dl * nx + dx]
        got_far[f, my_far] = total
        half_sum[f] = total
        for d in (2, 1, 3):
            f_copy(f, d).start()
    for f in range(nf):
        for d in range(1, nh):
            f_copy(f, d).wait_recv()
        total = got_far[f, 0]
        for i in range(1, nh):
            total = total + got_far[f, i]
        g_ref[f, chunk(my_near), :] = total
        for dl, dx in near:
            w_copy(f, dl, dx).start()
    for f in range(nf):
        for d in range(1, nt):
            a_copy(f, d).wait_send()
        for dl, dx in near:
            r_copy(f, dl, dx).wait_send()
        for d in range(1, nh):
            f_copy(f, d).wait_send()
    for f in range(nf):
        for dl, dx in near:
            w_copy(f, dl, dx).wait_recv()
    for f in range(nf):
        for dl, dx in near:
            w_copy(f, dl, dx).wait_send()


def exchange(snapshots, frequencies, offsets):
    nt = lax.axis_size("tm")
    nx, nl = 4, 4
    group = nx * nl
    nh = lax.axis_size("space") // group
    blocks, length, cells = snapshots.shape
    nf_all = frequencies.shape[0]
    nf, nb = nf_all // nt, blocks * nt
    wide = nb // group
    halves = cells // LANES
    vm = pl.BlockSpec(memory_space=pltpu.VMEM)
    dma = pltpu.SemaphoreType.DMA
    q, g = pl.pallas_call(
        functools.partial(exchange_kernel, nt, nx, nl, nh),
        out_shape=(jax.ShapeDtypeStruct((nf, 2, nb, cells), BF16), jax.ShapeDtypeStruct((nf, nb, nb), F32)),
        in_specs=[pl.BlockSpec(memory_space=pltpu.HBM)] * 3, out_specs=(vm, vm),
        scratch_shapes=[
            pltpu.SMEM((nf_all,), jnp.int32),
            pltpu.SMEM((blocks,), jnp.int32),
            pltpu.VMEM((blocks, length, cells), BF16),
            pltpu.VMEM((halves, blocks * 2 * nf_all, LANES), F32),
            pltpu.VMEM((nf, nt, 2, blocks, cells), BF16),
            pltpu.VMEM((nf, nb, nb), F32),
            pltpu.VMEM((nf, group, wide, nb), F32),
            pltpu.VMEM((nf, wide, nb), F32),
            pltpu.VMEM((nf, nh, wide, nb), F32),
            dma((6,)), dma((nf, nt)), dma((nf, nt)), dma((nf, group)), dma((nf, group)),
            dma((nf, nh)), dma((nf, nh)), dma((nf, group)), dma((nf, group)), dma((nf,)),
        ],
        compiler_params=pltpu.CompilerParams(
            collective_id=0, has_side_effects=True, vmem_limit_bytes=53 << 20),
        name="exchange_gram",
    )(*[pltpu.with_memory_space_constraint(a, pltpu.HBM) for a in (frequencies, offsets, snapshots)])
    return q, g


def split2(v):
    hi = v.astype(BF16)
    lo = (v - hi.astype(F32)).astype(BF16)
    return hi, lo


def lane_bcast(v, col):
    return jnp.broadcast_to(v[:, col:col + 1], v.shape)


def row_bcast(v, s):
    return jnp.broadcast_to(v[s:s + 1, :], v.shape)


def factor_kernel(scale, block, q_ref, g_ref, out_ref, m_re, m_im, w_ref):
    nf, _, nb, cells = q_ref.shape
    row8 = lax.broadcasted_iota(jnp.int32, (8, nb), 0)
    lane8 = lax.broadcasted_iota(jnp.int32, (8, nb), 1)
    row = lax.broadcasted_iota(jnp.int32, (nb, nb), 0)
    lane = lax.broadcasted_iota(jnp.int32, (nb, nb), 1)
    for f in range(nf):
        packed = g_ref[f] * scale
        flipped = packed.T
        m_re[f] = jnp.where(row >= lane, packed, flipped)
        m_im[f] = jnp.where(row > lane, -flipped, jnp.where(row < lane, packed, 0.0))
    per = block // 8
    for k in range(nb // block):
        r0 = k * block
        R = [
            [[m_re[f, r0 + 8 * v:r0 + 8 * v + 8, :] for v in range(per)],
             [m_im[f, r0 + 8 * v:r0 + 8 * v + 8, :] for v in range(per)]]
            for f in range(nf)
        ]
        dsel = [[jnp.ones((8, nb), F32) for v in range(per)] for f in range(nf)]
        for v0 in range(per):
            c0 = r0 + 8 * v0
            B = [
                [[[lane_bcast(R[f][ri][v], c0 + c) for c in range(8)] for v in range(v0, per)] for ri in range(2)]
                for f in range(nf)
            ]
            for s in range(8):
                at_col = lane8 == c0 + s
                below = row8 > s
                for f in range(nf):
                    re, im = R[f]
                    b_re, b_im = B[f]
                    d = row_bcast(b_re[0][s], s)
                    ninv = -1.0 / d
                    dsel[f][v0] = jnp.where(row8 == s, d, dsel[f][v0])
                    p_re, p_im = row_bcast(re[v0], s), row_bcast(im[v0], s)
                    h_re = [row_bcast(b_re[0][c], s) if c > s else None for c in range(8)]
                    h_im = [row_bcast(b_im[0][c], s) if c > s else None for c in range(8)]
                    for v in range(v0, per):
                        i = v - v0
                        if i == 0 and s == 7:
                            continue
                        n_re = b_re[i][s] * ninv
                        n_im = b_im[i][s] * ninv
                        if i == 0:
                            n_re = jnp.where(below, n_re, 0.0)
                            n_im = jnp.where(below, n_im, 0.0)
                        for c in range(s + 1, 8):
                            b_re[i][c], b_im[i][c] = (
                                b_re[i][c] + (n_re * h_re[c] - n_im * h_im[c]),
                                b_im[i][c] + (n_re * h_im[c] + n_im * h_re[c]),
                            )
                        re[v], im[v] = (
                            jnp.where(at_col, n_re, re[v] + (n_re * p_re - n_im * p_im)),
                            jnp.where(at_col, n_im, im[v] + (n_re * p_im + n_im * p_re)),
                        )
        for f in range(nf):
            re, im = R[f]
            n_re, n_im = [], []
            for v in range(per):
                mine = row8 + (r0 + 8 * v)
                rs = lax.rsqrt(dsel[f][v])
                cut = (lane8 > mine) & (lane8 < r0 + block)
                n_re.append(jnp.where(cut, 0.0, jnp.where(lane8 == mine, rs, re[v] * rs)))
                n_im.append(jnp.where(cut | (lane8 == mine), 0.0, im[v] * rs))
            a_re = jnp.concatenate(n_re, axis=0)
            a_im = jnp.concatenate(n_im, axis=0)
            keep = lax.broadcasted_iota(jnp.int32, (block, nb), 1) < r0 + block
            w_ref[f, 0, r0:r0 + block, :] = jnp.where(keep, a_re, 0.0)
            w_ref[f, 1, r0:r0 + block, :] = jnp.where(keep, a_im, 0.0)
            if k + 1 < nb // block:
                rest = nb - r0 - block
                rh, rl = split2(a_re)
                ih, il = split2(a_im)
                lcat = jnp.concatenate([rh, ih, rh, ih, rl, il], axis=0)
                rcat = jnp.concatenate(
                    [jnp.concatenate([rh, ih, rl, il, rh, ih], axis=0),
                     jnp.concatenate([ih, -rh, il, -rl, ih, -rh], axis=0)], axis=1)
                upd = lax.dot_general(lcat, rcat, (((0,), (0,)), ((), ())), preferred_element_type=F32)
                upd = upd[r0 + block:, :]
                inside = lax.broadcasted_iota(jnp.int32, (rest, nb), 1)
                inside = (inside >= r0) & (inside < r0 + block)
                m_re[f, r0 + block:, :] = jnp.where(inside, 0.0, m_re[f, r0 + block:, :]) - upd[:, :nb]
                m_im[f, r0 + block:, :] = jnp.where(inside, 0.0, m_im[f, r0 + block:, :]) - upd[:, nb:]
    for f in range(nf):
        w_re, w_im = w_ref[f, 0], w_ref[f, 1]
        rh, rl = split2(w_re)
        ih, il = split2(w_im)
        x_re, x_im = q_ref[f, 0], q_ref[f, 1]
        x = jnp.concatenate([x_re, x_im], axis=0)
        a = jnp.concatenate([rh, -ih], axis=1)
        al = jnp.concatenate([rl, -il], axis=1)
        b = jnp.concatenate([ih, rh], axis=1)
        bl = jnp.concatenate([il, rl], axis=1)
        out_ref[f, 0] = jnp.dot(a, x, preferred_element_type=F32) + jnp.dot(al, x, preferred_element_type=F32)
        out_ref[f, 1] = jnp.dot(b, x, preferred_element_type=F32) + jnp.dot(bl, x, preferred_element_type=F32)


def finish(q, g, scale, block=16):
    nf, _, nb, cells = q.shape
    vm = pl.BlockSpec(memory_space=pltpu.VMEM)
    return pl.pallas_call(
        functools.partial(factor_kernel, scale, block),
        out_shape=jax.ShapeDtypeStruct((nf, 2, nb, cells), F32),
        in_specs=[vm, vm], out_specs=vm,
        scratch_shapes=[pltpu.VMEM((nf, nb, nb), F32), pltpu.VMEM((nf, nb, nb), F32), pltpu.VMEM((nf, 2, nb, nb), F32)],
        compiler_params=pltpu.CompilerParams(vmem_limit_bytes=32 << 20),
        name="factor_apply",
    )(q, g)


def local(snapshots, frequencies, offsets):
    total_cells = snapshots.shape[2] * lax.axis_size("space")
    q, g = exchange(snapshots, frequencies, offsets)
    return finish(q, g, 1.0 / total_cells)


def solution(mesh):
    placed = (P("tm", None, "space"), P(), P("tm"))
    return jax.shard_map(
        local, mesh=mesh, in_specs=placed, out_specs=P("tm", None, None, "space"), check_vma=False
    )
```

```python
import functools
import math

import jax
import jax.numpy as jnp
from jax import lax
from jax.experimental import pallas as pl
from jax.experimental.pallas import tpu as pltpu
from jax.sharding import PartitionSpec as P

F32 = jnp.float32
BF16 = jnp.bfloat16

MESH = pl.DeviceIdType.MESH
LANES = 128


def cos_sin(turns, length):
    quarter = length // 4
    shifted = turns + quarter // 2
    quadrant = lax.rem(lax.div(shifted, quarter), 4)
    theta = (lax.rem(shifted, quarter) - quarter // 2).astype(F32) * (2.0 * math.pi / length)
    sq = theta * theta
    cos_small = 1.0 + sq * (-0.5 + sq * (1 / 24 + sq * (-1 / 720 + sq * (1 / 40320 - sq / 3628800))))
    sin_small = theta * (1.0 + sq * (-1 / 6 + sq * (1 / 120 + sq * (-1 / 5040 + sq / 362880))))
    swap = (quadrant == 1) | (quadrant == 3)
    cos_sign = jnp.where((quadrant == 1) | (quadrant == 2), -1.0, 1.0)
    sin_sign = jnp.where(quadrant >= 2, -1.0, 1.0)
    return (
        jnp.where(swap, sin_small, cos_small) * cos_sign,
        jnp.where(swap, cos_small, sin_small) * sin_sign,
    )


def exchange_kernel(
    nt, nx, nl, nh, freq_hbm, off_hbm, snap_hbm, q_ref, g_ref,
    freq_ref, off_ref, snap, work, send, part, got, half_sum, got_far, final,
    far_ok, in_sem, a_send, a_recv, r_send, r_recv, f_send, f_recv, w_send, w_recv, own_sem,
):
    nf_all = freq_ref.shape[0]
    blocks, length, cells = snap.shape
    nf = nf_all // nt
    nb = blocks * nt
    halves = cells // LANES
    group = nx * nl
    me = lax.axis_index("tm")
    spot = lax.axis_index("space")
    my_far = lax.div(spot, group)
    my_near = lax.rem(spot, group)
    my_l = lax.div(my_near, nx)
    my_x = lax.rem(my_near, nx)
    my_y = lax.div(me, 2)
    core = lax.rem(me, 2)
    owns = core * lax.div(lax.rem(my_l + 1, nl), 2)
    flip = lax.div(my_far, 2)
    my_m = (my_l - 1) + flip * (3 - 2 * my_l)

    def tm_peer(d):
        return (lax.rem(me + d, nt), spot)

    def plane(far, m):
        return 1 + m + lax.div(far, 2) * (1 - 2 * m)

    def owner(m, dx):
        return (2 * my_y + 1, my_far * group + plane(my_far, m) * nx + lax.rem(my_x + dx, nx))

    def not_me(m, dx):
        return (core == 0) | (my_l != plane(my_far, m)) if dx == 0 else my_x >= 0

    def client(c, dl, dx):
        return (2 * my_y + c, my_far * group + lax.rem(my_l + dl, nl) * nx + lax.rem(my_x + dx, nx))

    def far_owner(d):
        far = lax.rem(my_far + d, nh)
        return (me, far * group + plane(far, my_m) * nx + my_x)

    def rank(far):
        return far + lax.div(far, 2) * (5 - 2 * far)

    my_rank = rank(my_far)

    def far_rank(d):
        return rank(lax.rem(my_far + d, nh))

    order = (2, 1, 3, 0)
    targets = [(m, dx) for dx in order for m in range(2)]
    clients = [(c, dl, dx) for dx in order for dl in order for c in range(2) if dl or dx or c == 0]

    barrier = pltpu.get_barrier_semaphore()

    @pl.when(owns == 1)
    def _():
        for d in range(1, nh):
            @pl.when(far_rank(d) > my_rank)
            def _():
                pl.semaphore_signal(barrier, inc=1, device_id=far_owner(d), device_id_type=MESH)
        for c, dl, dx in clients:
            pl.semaphore_signal(barrier, inc=1, device_id=client(c, dl, dx), device_id_type=MESH)

    for m, dx in targets:
        @pl.when(not_me(m, dx))
        def _():
            pl.semaphore_signal(barrier, inc=1, device_id=owner(m, dx), device_id_type=MESH)

    for d in range(1, nt):
        pl.semaphore_signal(barrier, inc=1, device_id=tm_peer(d), device_id_type=MESH)

    small = [
        pltpu.make_async_copy(freq_hbm, freq_ref, in_sem.at[4]),
        pltpu.make_async_copy(off_hbm, off_ref, in_sem.at[5]),
    ]
    for load in small:
        load.start()
    step = blocks // 4
    loads = [
        pltpu.make_async_copy(snap_hbm.at[pl.ds(i * step, step)], snap.at[pl.ds(i * step, step)], in_sem.at[i])
        for i in range(4)
    ]
    for load in loads:
        load.start()

    row = lax.broadcasted_iota(jnp.int32, (nf_all, length), 0)
    position = lax.broadcasted_iota(jnp.int32, (nf_all, length), 1)
    for load in small:
        load.wait()
    freq = jnp.zeros((nf_all, length), jnp.int32)
    start = jnp.zeros((nf_all, length), jnp.int32)
    for j in range(nf_all):
        freq = jnp.where(row == j, freq_ref[j], freq)
    for b in range(blocks):
        start = jnp.where(position == b, off_ref[b], start)
    window = 0.5 - 0.5 * cos_sin(position, length)[0]
    cosine, sine = cos_sin(lax.rem(freq * position, length), length)
    table = jnp.concatenate([window * cosine, window * sine], axis=0).astype(BF16)
    cos_phase, sin_phase = cos_sin(lax.rem(freq * lax.rem(start, length), length), length)

    for b in range(blocks):
        if b % step == 0:
            loads[b // step].wait()
        both = jnp.dot(table, snap[b], preferred_element_type=F32)
        cos_part, sin_part = both[:nf_all], both[nf_all:]
        cp, sp = cos_phase[:, b:b + 1], sin_phase[:, b:b + 1]
        base = b * 2 * nf_all
        real = cos_part * cp - sin_part * sp
        imag = -(sin_part * cp + cos_part * sp)
        for h in range(halves):
            work[h, base:base + nf_all, :] = real[:, h * LANES:(h + 1) * LANES]
            work[h, base + nf_all:base + 2 * nf_all, :] = imag[:, h * LANES:(h + 1) * LANES]

    mine = pl.ds(pl.multiple_of(me * blocks, blocks), blocks)

    def a_copy(f, d):
        return pltpu.make_async_remote_copy(
            src_ref=send.at[f, lax.rem(me + d, nt)],
            dst_ref=q_ref.at[f, :, mine, :],
            send_sem=a_send.at[f, d], recv_sem=a_recv.at[f, d],
            device_id=tm_peer(d), device_id_type=MESH)

    own = [pltpu.make_async_copy(send.at[f, me], q_ref.at[f, :, mine, :], own_sem.at[f]) for f in range(nf)]
    for f in range(nf):
        for t in range(nt):
            for ri in range(2):
                for h in range(halves):
                    rows = work[h, pl.ds(ri * nf_all + t * nf + f, blocks, stride=2 * nf_all), :]
                    send[f, t, ri, :, h * LANES:(h + 1) * LANES] = rows.astype(BF16)
        if f == 0:
            pl.semaphore_wait(barrier, nt - 1 + 2 * nx + owns * (len(clients) - 1 + my_rank))
        for d in (4, 3, 5, 2, 6, 1, 7):
            a_copy(f, d).start()
        own[f].start()

    @pl.when(owns == 1)
    def _():
        for d in range(1, nh):
            @pl.when(far_rank(d) < my_rank)
            def _():
                pl.semaphore_signal(far_ok.at[nh - d], inc=1, device_id=far_owner(d), device_id_type=MESH)

    grow = lax.broadcasted_iota(jnp.int32, (nb, nb), 0)
    glane = lax.broadcasted_iota(jnp.int32, (nb, nb), 1)
    wide = nb // (2 * nx)

    def chunk(m, x):
        return pl.ds(pl.multiple_of((m * nx + x) * wide, wide), wide)

    for f in range(nf):
        own[f].wait()
        for d in range(1, nt):
            a_copy(f, d).wait_recv()
        rows = q_ref[f].reshape(2 * nb, cells)
        full = lax.dot_general(rows, rows, (((1,), (1,)), ((), ())), preferred_element_type=F32)
        real = full[:nb, :nb] + full[nb:, nb:]
        imag = full[nb:, :nb] - full[:nb, nb:]
        part[f] = jnp.where(grow >= glane, real, imag)

    def r_copy(m, dx):
        spot_there = lax.rem(my_l - plane(my_far, m) + nl, nl) * nx + (nx - dx) % nx
        return pltpu.make_async_remote_copy(
            src_ref=part.at[:, chunk(m, lax.rem(my_x + dx, nx)), :], dst_ref=got.at[core, spot_there],
            send_sem=r_send.at[m, dx], recv_sem=r_recv.at[core, spot_there],
            device_id=owner(m, dx), device_id_type=MESH)

    for m, dx in targets:
        @pl.when(not_me(m, dx))
        def _():
            r_copy(m, dx).start()

    my_chunk = chunk(my_m, my_x)

    def r_arrival(c, i):
        return pltpu.make_async_remote_copy(
            src_ref=half_sum.at[0], dst_ref=got.at[c, i], send_sem=r_send.at[0, 0], recv_sem=r_recv.at[c, i],
            device_id=tm_peer(1), device_id_type=MESH)

    def f_copy(d):
        return pltpu.make_async_remote_copy(
            src_ref=half_sum, dst_ref=got_far.at[my_far],
            send_sem=f_send.at[d], recv_sem=f_recv.at[d],
            device_id=far_owner(d), device_id_type=MESH)

    def w_copy(c, dl, dx):
        return pltpu.make_async_remote_copy(
            src_ref=final.at[c], dst_ref=g_ref.at[:, my_chunk, :],
            send_sem=w_send.at[c, dl * nx + dx], recv_sem=w_recv.at[my_m * nx + my_x],
            device_id=client(c, dl, dx), device_id_type=MESH)

    @pl.when(owns == 1)
    def _():
        for c in range(2):
            total = part[:, my_chunk, :] if c == 1 else None
            for i in range(group):
                if c == 0 or i > 0:
                    r_arrival(c, i).wait_recv()
                    total = got[c, i] if total is None else total + got[c, i]
            half_sum[c] = total
            got_far[my_far, c] = total
        for d in (2, 1, 3):
            @pl.when(far_rank(d) < my_rank)
            def _():
                f_copy(d).start()
        for d in (1, 3, 2):
            @pl.when(far_rank(d) > my_rank)
            def _():
                pl.semaphore_wait(far_ok.at[d], 1)
                f_copy(d).start()
        for d in (1, 3, 2):
            f_copy(d).wait_recv()
        for c in range(2):
            total = got_far[0, c]
            for i in range(1, nh):
                total = total + got_far[i, c]
            final[c] = total
        for c, dl, dx in clients:
            w_copy(c, dl, dx).start()
        g_ref[:, my_chunk, :] = final[1]

    def w_arrival(slot):
        return pltpu.make_async_remote_copy(
            src_ref=final.at[0], dst_ref=g_ref.at[:, pl.ds(slot * wide, wide), :],
            send_sem=w_send.at[0, 0], recv_sem=w_recv.at[slot],
            device_id=tm_peer(1), device_id_type=MESH)

    for slot in range(2 * nx):
        @pl.when((owns == 0) | (my_m * nx + my_x != slot))
        def _():
            w_arrival(slot).wait_recv()

    for f in range(nf):
        for d in range(1, nt):
            a_copy(f, d).wait_send()
    for m, dx in targets:
        @pl.when(not_me(m, dx))
        def _():
            r_copy(m, dx).wait_send()

    @pl.when(owns == 1)
    def _():
        for d in range(1, nh):
            f_copy(d).wait_send()
        for c, dl, dx in clients:
            w_copy(c, dl, dx).wait_send()


def exchange(snapshots, frequencies, offsets):
    nt = lax.axis_size("tm")
    nx, nl = 4, 4
    group = nx * nl
    nh = lax.axis_size("space") // group
    blocks, length, cells = snapshots.shape
    nf_all = frequencies.shape[0]
    nf, nb = nf_all // nt, blocks * nt
    wide = nb // (2 * nx)
    halves = cells // LANES
    vm = pl.BlockSpec(memory_space=pltpu.VMEM)
    dma = pltpu.SemaphoreType.DMA
    q, g = pl.pallas_call(
        functools.partial(exchange_kernel, nt, nx, nl, nh),
        out_shape=(jax.ShapeDtypeStruct((nf, 2, nb, cells), BF16), jax.ShapeDtypeStruct((nf, nb, nb), F32)),
        in_specs=[pl.BlockSpec(memory_space=pltpu.HBM)] * 3, out_specs=(vm, vm),
        scratch_shapes=[
            pltpu.SMEM((nf_all,), jnp.int32),
            pltpu.SMEM((blocks,), jnp.int32),
            pltpu.VMEM((blocks, length, cells), BF16),
            pltpu.VMEM((halves, blocks * 2 * nf_all, LANES), F32),
            pltpu.VMEM((nf, nt, 2, blocks, cells), BF16),
            pltpu.VMEM((nf, nb, nb), F32),
            pltpu.VMEM((2, group, nf, wide, nb), F32),
            pltpu.VMEM((2, nf, wide, nb), F32),
            pltpu.VMEM((nh, 2, nf, wide, nb), F32),
            pltpu.VMEM((2, nf, wide, nb), F32),
            pltpu.SemaphoreType.REGULAR((nh,)), dma((6,)), dma((nf, nt)), dma((nf, nt)), dma((2, nx)), dma((2, group)),
            dma((nh,)), dma((nh,)), dma((2, group)), dma((2 * nx,)), dma((nf,)),
        ],
        compiler_params=pltpu.CompilerParams(
            collective_id=0, has_side_effects=True, vmem_limit_bytes=53 << 20),
        name="exchange_gram",
    )(*[pltpu.with_memory_space_constraint(a, pltpu.HBM) for a in (frequencies, offsets, snapshots)])
    return q, g


def split2(v):
    hi = v.astype(BF16)
    lo = (v - hi.astype(F32)).astype(BF16)
    return hi, lo


def lane_bcast(v, col):
    return jnp.broadcast_to(v[:, col:col + 1], v.shape)


def row_bcast(v, s):
    return jnp.broadcast_to(v[s:s + 1, :], v.shape)


def factor_kernel(scale, block, q_ref, g_ref, out_ref, m_re, m_im, w_ref):
    nf, _, nb, cells = q_ref.shape
    row8 = lax.broadcasted_iota(jnp.int32, (8, nb), 0)
    lane8 = lax.broadcasted_iota(jnp.int32, (8, nb), 1)
    row = lax.broadcasted_iota(jnp.int32, (nb, nb), 0)
    lane = lax.broadcasted_iota(jnp.int32, (nb, nb), 1)
    for f in range(nf):
        packed = g_ref[f] * scale
        flipped = packed.T
        m_re[f] = jnp.where(row >= lane, packed, flipped)
        m_im[f] = jnp.where(row > lane, -flipped, jnp.where(row < lane, packed, 0.0))
    per = block // 8
    for k in range(nb // block):
        r0 = k * block
        R = [
            [[m_re[f, r0 + 8 * v:r0 + 8 * v + 8, :] for v in range(per)],
             [m_im[f, r0 + 8 * v:r0 + 8 * v + 8, :] for v in range(per)]]
            for f in range(nf)
        ]
        dsel = [[jnp.ones((8, nb), F32) for v in range(per)] for f in range(nf)]
        for v0 in range(per):
            c0 = r0 + 8 * v0
            B = [
                [[[lane_bcast(R[f][ri][v], c0 + c) for c in range(8)] for v in range(v0, per)] for ri in range(2)]
                for f in range(nf)
            ]
            for s in range(8):
                at_col = lane8 == c0 + s
                below = row8 > s
                for f in range(nf):
                    re, im = R[f]
                    b_re, b_im = B[f]
                    d = row_bcast(b_re[0][s], s)
                    ninv = -1.0 / d
                    dsel[f][v0] = jnp.where(row8 == s, d, dsel[f][v0])
                    p_re, p_im = row_bcast(re[v0], s), row_bcast(im[v0], s)
                    h_re = [row_bcast(b_re[0][c], s) if c > s else None for c in range(8)]
                    h_im = [row_bcast(b_im[0][c], s) if c > s else None for c in range(8)]
                    for v in range(v0, per):
                        i = v - v0
                        if i == 0 and s == 7:
                            continue
                        n_re = b_re[i][s] * ninv
                        n_im = b_im[i][s] * ninv
                        if i == 0:
                            n_re = jnp.where(below, n_re, 0.0)
                            n_im = jnp.where(below, n_im, 0.0)
                        for c in range(s + 1, 8):
                            b_re[i][c], b_im[i][c] = (
                                b_re[i][c] + (n_re * h_re[c] - n_im * h_im[c]),
                                b_im[i][c] + (n_re * h_im[c] + n_im * h_re[c]),
                            )
                        re[v], im[v] = (
                            jnp.where(at_col, n_re, re[v] + (n_re * p_re - n_im * p_im)),
                            jnp.where(at_col, n_im, im[v] + (n_re * p_im + n_im * p_re)),
                        )
        for f in range(nf):
            re, im = R[f]
            n_re, n_im = [], []
            for v in range(per):
                mine = row8 + (r0 + 8 * v)
                rs = lax.rsqrt(dsel[f][v])
                cut = (lane8 > mine) & (lane8 < r0 + block)
                n_re.append(jnp.where(cut, 0.0, jnp.where(lane8 == mine, rs, re[v] * rs)))
                n_im.append(jnp.where(cut | (lane8 == mine), 0.0, im[v] * rs))
            a_re = jnp.concatenate(n_re, axis=0)
            a_im = jnp.concatenate(n_im, axis=0)
            keep = lax.broadcasted_iota(jnp.int32, (block, nb), 1) < r0 + block
            w_ref[f, 0, r0:r0 + block, :] = jnp.where(keep, a_re, 0.0)
            w_ref[f, 1, r0:r0 + block, :] = jnp.where(keep, a_im, 0.0)
            if k + 1 < nb // block:
                rest = nb - r0 - block
                rh, rl = split2(a_re)
                ih, il = split2(a_im)
                lcat = jnp.concatenate([rh, ih, rh, ih, rl, il], axis=0)
                rcat = jnp.concatenate(
                    [jnp.concatenate([rh, ih, rl, il, rh, ih], axis=0),
                     jnp.concatenate([ih, -rh, il, -rl, ih, -rh], axis=0)], axis=1)
                upd = lax.dot_general(lcat, rcat, (((0,), (0,)), ((), ())), preferred_element_type=F32)
                upd = upd[r0 + block:, :]
                inside = lax.broadcasted_iota(jnp.int32, (rest, nb), 1)
                inside = (inside >= r0) & (inside < r0 + block)
                m_re[f, r0 + block:, :] = jnp.where(inside, 0.0, m_re[f, r0 + block:, :]) - upd[:, :nb]
                m_im[f, r0 + block:, :] = jnp.where(inside, 0.0, m_im[f, r0 + block:, :]) - upd[:, nb:]
    for f in range(nf):
        w_re, w_im = w_ref[f, 0], w_ref[f, 1]
        rh, rl = split2(w_re)
        ih, il = split2(w_im)
        x_re, x_im = q_ref[f, 0], q_ref[f, 1]
        x = jnp.concatenate([x_re, x_im], axis=0)
        a = jnp.concatenate([rh, -ih], axis=1)
        al = jnp.concatenate([rl, -il], axis=1)
        b = jnp.concatenate([ih, rh], axis=1)
        bl = jnp.concatenate([il, rl], axis=1)
        out_ref[f, 0] = jnp.dot(a, x, preferred_element_type=F32) + jnp.dot(al, x, preferred_element_type=F32)
        out_ref[f, 1] = jnp.dot(b, x, preferred_element_type=F32) + jnp.dot(bl, x, preferred_element_type=F32)


def finish(q, g, scale, block=16):
    nf, _, nb, cells = q.shape
    vm = pl.BlockSpec(memory_space=pltpu.VMEM)
    return pl.pallas_call(
        functools.partial(factor_kernel, scale, block),
        out_shape=jax.ShapeDtypeStruct((nf, 2, nb, cells), F32),
        in_specs=[vm, vm], out_specs=vm,
        scratch_shapes=[pltpu.VMEM((nf, nb, nb), F32), pltpu.VMEM((nf, nb, nb), F32), pltpu.VMEM((nf, 2, nb, nb), F32)],
        compiler_params=pltpu.CompilerParams(vmem_limit_bytes=32 << 20),
        name="factor_apply",
    )(q, g)


def local(snapshots, frequencies, offsets):
    total_cells = snapshots.shape[2] * lax.axis_size("space")
    q, g = exchange(snapshots, frequencies, offsets)
    return finish(q, g, 1.0 / total_cells)


def solution(mesh):
    placed = (P("tm", None, "space"), P(), P("tm"))
    return jax.shard_map(
        local, mesh=mesh, in_specs=placed, out_specs=P("tm", None, None, "space"), check_vma=False
    )
```

```python
import functools
import math

import jax
import jax.numpy as jnp
from jax import lax
from jax.experimental import pallas as pl
from jax.experimental.pallas import tpu as pltpu
from jax.sharding import PartitionSpec as P

F32 = jnp.float32
BF16 = jnp.bfloat16

MESH = pl.DeviceIdType.MESH
LANES = 128


def cos_sin(turns, length):
    quarter = length // 4
    shifted = turns + quarter // 2
    quadrant = lax.rem(lax.div(shifted, quarter), 4)
    theta = (lax.rem(shifted, quarter) - quarter // 2).astype(F32) * (2.0 * math.pi / length)
    sq = theta * theta
    cos_small = 1.0 + sq * (-0.5 + sq * (1 / 24 + sq * (-1 / 720 + sq * (1 / 40320 - sq / 3628800))))
    sin_small = theta * (1.0 + sq * (-1 / 6 + sq * (1 / 120 + sq * (-1 / 5040 + sq / 362880))))
    swap = (quadrant == 1) | (quadrant == 3)
    cos_sign = jnp.where((quadrant == 1) | (quadrant == 2), -1.0, 1.0)
    sin_sign = jnp.where(quadrant >= 2, -1.0, 1.0)
    return (
        jnp.where(swap, sin_small, cos_small) * cos_sign,
        jnp.where(swap, cos_small, sin_small) * sin_sign,
    )


def exchange_kernel(
    nt, nx, nl, nh, freq_hbm, off_hbm, snap_hbm, q_ref, g_ref,
    freq_ref, off_ref, snap, work, send, part, got, half_sum, got_far, final,
    far_ok, in_sem, a_send, a_recv, r_send, r_recv, f_send, f_recv, w_send, w_recv, own_sem,
):
    nf_all = freq_ref.shape[0]
    blocks, length, cells = snap.shape
    nf = nf_all // nt
    nb = blocks * nt
    halves = cells // LANES
    group = nx * nl
    me = lax.axis_index("tm")
    spot = lax.axis_index("space")
    my_far = lax.div(spot, group)
    my_near = lax.rem(spot, group)
    my_l = lax.div(my_near, nx)
    my_x = lax.rem(my_near, nx)
    my_y = lax.div(me, 2)
    core = lax.rem(me, 2)
    owns = core * lax.div(lax.rem(my_l + 1, nl), 2)
    flip = lax.div(my_far, 2)
    my_m = (my_l - 1) + flip * (3 - 2 * my_l)

    def tm_peer(d):
        return (lax.rem(me + d, nt), spot)

    def plane(far, m):
        return 1 + m + lax.div(far, 2) * (1 - 2 * m)

    def owner(m, dx):
        return (2 * my_y + 1, my_far * group + plane(my_far, m) * nx + lax.rem(my_x + dx, nx))

    def not_me(m, dx):
        return (core == 0) | (my_l != plane(my_far, m)) if dx == 0 else my_x >= 0

    def client(c, dl, dx):
        return (2 * my_y + c, my_far * group + lax.rem(my_l + dl, nl) * nx + lax.rem(my_x + dx, nx))

    def far_owner(d):
        far = lax.rem(my_far + d, nh)
        return (me, far * group + plane(far, my_m) * nx + my_x)

    def rank(far):
        return far + lax.div(far, 2) * (5 - 2 * far)

    my_rank = rank(my_far)

    def far_rank(d):
        return rank(lax.rem(my_far + d, nh))

    order = (2, 1, 3, 0)
    targets = [(m, dx) for dx in order for m in range(2)]
    clients = [(c, dl, dx) for c in (1, 0) for dx in order for dl in order if dl or dx or c == 0]

    barrier = pltpu.get_barrier_semaphore()

    @pl.when(owns == 1)
    def _():
        for d in range(1, nh):
            @pl.when(far_rank(d) > my_rank)
            def _():
                pl.semaphore_signal(barrier, inc=1, device_id=far_owner(d), device_id_type=MESH)
        for c, dl, dx in clients:
            pl.semaphore_signal(barrier, inc=1, device_id=client(c, dl, dx), device_id_type=MESH)

    for m, dx in targets:
        @pl.when(not_me(m, dx))
        def _():
            pl.semaphore_signal(barrier, inc=1, device_id=owner(m, dx), device_id_type=MESH)

    for d in range(1, nt):
        pl.semaphore_signal(barrier, inc=1, device_id=tm_peer(d), device_id_type=MESH)

    small = [
        pltpu.make_async_copy(freq_hbm, freq_ref, in_sem.at[4]),
        pltpu.make_async_copy(off_hbm, off_ref, in_sem.at[5]),
    ]
    for load in small:
        load.start()
    step = blocks // 4
    loads = [
        pltpu.make_async_copy(snap_hbm.at[pl.ds(i * step, step)], snap.at[pl.ds(i * step, step)], in_sem.at[i])
        for i in range(4)
    ]
    for load in loads:
        load.start()

    row = lax.broadcasted_iota(jnp.int32, (nf_all, length), 0)
    position = lax.broadcasted_iota(jnp.int32, (nf_all, length), 1)
    for load in small:
        load.wait()
    freq = jnp.zeros((nf_all, length), jnp.int32)
    start = jnp.zeros((nf_all, length), jnp.int32)
    for j in range(nf_all):
        freq = jnp.where(row == j, freq_ref[j], freq)
    for b in range(blocks):
        start = jnp.where(position == b, off_ref[b], start)
    window = 0.5 - 0.5 * cos_sin(position, length)[0]
    cosine, sine = cos_sin(lax.rem(freq * position, length), length)
    table = jnp.concatenate([window * cosine, window * sine], axis=0).astype(BF16)
    cos_phase, sin_phase = cos_sin(lax.rem(freq * lax.rem(start, length), length), length)

    for b in range(blocks):
        if b % step == 0:
            loads[b // step].wait()
        both = jnp.dot(table, snap[b], preferred_element_type=F32)
        cos_part, sin_part = both[:nf_all], both[nf_all:]
        cp, sp = cos_phase[:, b:b + 1], sin_phase[:, b:b + 1]
        base = b * 2 * nf_all
        real = cos_part * cp - sin_part * sp
        imag = -(sin_part * cp + cos_part * sp)
        for h in range(halves):
            work[h, base:base + nf_all, :] = real[:, h * LANES:(h + 1) * LANES]
            work[h, base + nf_all:base + 2 * nf_all, :] = imag[:, h * LANES:(h + 1) * LANES]

    mine = pl.ds(pl.multiple_of(me * blocks, blocks), blocks)

    def a_copy(f, d):
        return pltpu.make_async_remote_copy(
            src_ref=send.at[f, lax.rem(me + d, nt)],
            dst_ref=q_ref.at[f, :, mine, :],
            send_sem=a_send.at[f, d], recv_sem=a_recv.at[f, d],
            device_id=tm_peer(d), device_id_type=MESH)

    own = [pltpu.make_async_copy(send.at[f, me], q_ref.at[f, :, mine, :], own_sem.at[f]) for f in range(nf)]
    for f in range(nf):
        for t in range(nt):
            for ri in range(2):
                for h in range(halves):
                    rows = work[h, pl.ds(ri * nf_all + t * nf + f, blocks, stride=2 * nf_all), :]
                    send[f, t, ri, :, h * LANES:(h + 1) * LANES] = rows.astype(BF16)
        if f == 0:
            pl.semaphore_wait(barrier, nt - 1 + 2 * nx + owns * (len(clients) - 1 + my_rank))
        for d in (4, 3, 5, 2, 6, 1, 7):
            a_copy(f, d).start()
        own[f].start()

    @pl.when(owns == 1)
    def _():
        for d in range(1, nh):
            @pl.when(far_rank(d) < my_rank)
            def _():
                pl.semaphore_signal(far_ok.at[nh - d], inc=1, device_id=far_owner(d), device_id_type=MESH)

    grow = lax.broadcasted_iota(jnp.int32, (nb, nb), 0)
    glane = lax.broadcasted_iota(jnp.int32, (nb, nb), 1)
    wide = nb // (2 * nx)

    def chunk(m, x):
        return pl.ds(pl.multiple_of((m * nx + x) * wide, wide), wide)

    for f in range(nf):
        own[f].wait()
        for d in range(1, nt):
            a_copy(f, d).wait_recv()
        rows = q_ref[f].reshape(2 * nb, cells)
        full = lax.dot_general(rows, rows, (((1,), (1,)), ((), ())), preferred_element_type=F32)
        real = full[:nb, :nb] + full[nb:, nb:]
        imag = full[nb:, :nb] - full[:nb, nb:]
        part[f] = jnp.where(grow >= glane, real, imag)

    def r_copy(m, dx):
        spot_there = lax.rem(my_l - plane(my_far, m) + nl, nl) * nx + (nx - dx) % nx
        return pltpu.make_async_remote_copy(
            src_ref=part.at[:, chunk(m, lax.rem(my_x + dx, nx)), :], dst_ref=got.at[core, spot_there],
            send_sem=r_send.at[m, dx], recv_sem=r_recv.at[core, spot_there],
            device_id=owner(m, dx), device_id_type=MESH)

    for m, dx in targets:
        @pl.when(not_me(m, dx))
        def _():
            r_copy(m, dx).start()

    my_chunk = chunk(my_m, my_x)

    def r_arrival(c, i):
        return pltpu.make_async_remote_copy(
            src_ref=half_sum.at[0], dst_ref=got.at[c, i], send_sem=r_send.at[0, 0], recv_sem=r_recv.at[c, i],
            device_id=tm_peer(1), device_id_type=MESH)

    def f_copy(d):
        return pltpu.make_async_remote_copy(
            src_ref=half_sum, dst_ref=got_far.at[my_far],
            send_sem=f_send.at[d], recv_sem=f_recv.at[d],
            device_id=far_owner(d), device_id_type=MESH)

    def w_copy(c, dl, dx):
        return pltpu.make_async_remote_copy(
            src_ref=final.at[c], dst_ref=g_ref.at[:, my_chunk, :],
            send_sem=w_send.at[c, dl * nx + dx], recv_sem=w_recv.at[my_m * nx + my_x],
            device_id=client(c, dl, dx), device_id_type=MESH)

    @pl.when(owns == 1)
    def _():
        for c in range(2):
            total = part[:, my_chunk, :] if c == 1 else None
            for i in range(group):
                if c == 0 or i > 0:
                    r_arrival(c, i).wait_recv()
                    total = got[c, i] if total is None else total + got[c, i]
            half_sum[c] = total
            got_far[my_far, c] = total
        for d in (2, 1, 3):
            @pl.when(far_rank(d) < my_rank)
            def _():
                f_copy(d).start()
        for d in (1, 3, 2):
            @pl.when(far_rank(d) > my_rank)
            def _():
                pl.semaphore_wait(far_ok.at[d], 1)
                f_copy(d).start()
        for d in (1, 3, 2):
            f_copy(d).wait_recv()
        for c in range(2):
            total = got_far[0, c]
            for i in range(1, nh):
                total = total + got_far[i, c]
            final[c] = total
        for c, dl, dx in clients:
            w_copy(c, dl, dx).start()
        g_ref[:, my_chunk, :] = final[1]

    def w_arrival(slot):
        return pltpu.make_async_remote_copy(
            src_ref=final.at[0], dst_ref=g_ref.at[:, pl.ds(slot * wide, wide), :],
            send_sem=w_send.at[0, 0], recv_sem=w_recv.at[slot],
            device_id=tm_peer(1), device_id_type=MESH)

    for slot in range(2 * nx):
        @pl.when((owns == 0) | (my_m * nx + my_x != slot))
        def _():
            w_arrival(slot).wait_recv()

    for f in range(nf):
        for d in range(1, nt):
            a_copy(f, d).wait_send()
    for m, dx in targets:
        @pl.when(not_me(m, dx))
        def _():
            r_copy(m, dx).wait_send()

    @pl.when(owns == 1)
    def _():
        for d in range(1, nh):
            f_copy(d).wait_send()
        for c, dl, dx in clients:
            w_copy(c, dl, dx).wait_send()


def exchange(snapshots, frequencies, offsets):
    nt = lax.axis_size("tm")
    nx, nl = 4, 4
    group = nx * nl
    nh = lax.axis_size("space") // group
    blocks, length, cells = snapshots.shape
    nf_all = frequencies.shape[0]
    nf, nb = nf_all // nt, blocks * nt
    wide = nb // (2 * nx)
    halves = cells // LANES
    vm = pl.BlockSpec(memory_space=pltpu.VMEM)
    dma = pltpu.SemaphoreType.DMA
    q, g = pl.pallas_call(
        functools.partial(exchange_kernel, nt, nx, nl, nh),
        out_shape=(jax.ShapeDtypeStruct((nf, 2, nb, cells), BF16), jax.ShapeDtypeStruct((nf, nb, nb), F32)),
        in_specs=[pl.BlockSpec(memory_space=pltpu.HBM)] * 3, out_specs=(vm, vm),
        scratch_shapes=[
            pltpu.SMEM((nf_all,), jnp.int32),
            pltpu.SMEM((blocks,), jnp.int32),
            pltpu.VMEM((blocks, length, cells), BF16),
            pltpu.VMEM((halves, blocks * 2 * nf_all, LANES), F32),
            pltpu.VMEM((nf, nt, 2, blocks, cells), BF16),
            pltpu.VMEM((nf, nb, nb), F32),
            pltpu.VMEM((2, group, nf, wide, nb), F32),
            pltpu.VMEM((2, nf, wide, nb), F32),
            pltpu.VMEM((nh, 2, nf, wide, nb), F32),
            pltpu.VMEM((2, nf, wide, nb), F32),
            pltpu.SemaphoreType.REGULAR((nh,)), dma((6,)), dma((nf, nt)), dma((nf, nt)), dma((2, nx)), dma((2, group)),
            dma((nh,)), dma((nh,)), dma((2, group)), dma((2 * nx,)), dma((nf,)),
        ],
        compiler_params=pltpu.CompilerParams(
            collective_id=0, has_side_effects=True, vmem_limit_bytes=53 << 20),
        name="exchange_gram",
    )(*[pltpu.with_memory_space_constraint(a, pltpu.HBM) for a in (frequencies, offsets, snapshots)])
    return q, g


def split2(v):
    hi = v.astype(BF16)
    lo = (v - hi.astype(F32)).astype(BF16)
    return hi, lo


def lane_bcast(v, col):
    return jnp.broadcast_to(v[:, col:col + 1], v.shape)


def row_bcast(v, s):
    return jnp.broadcast_to(v[s:s + 1, :], v.shape)


def factor_kernel(scale, block, q_ref, g_ref, out_ref, m_re, m_im, w_ref):
    nf, _, nb, cells = q_ref.shape
    row8 = lax.broadcasted_iota(jnp.int32, (8, nb), 0)
    lane8 = lax.broadcasted_iota(jnp.int32, (8, nb), 1)
    row = lax.broadcasted_iota(jnp.int32, (nb, nb), 0)
    lane = lax.broadcasted_iota(jnp.int32, (nb, nb), 1)
    for f in range(nf):
        packed = g_ref[f] * scale
        flipped = packed.T
        m_re[f] = jnp.where(row >= lane, packed, flipped)
        m_im[f] = jnp.where(row > lane, -flipped, jnp.where(row < lane, packed, 0.0))
    per = block // 8
    for k in range(nb // block):
        r0 = k * block
        R = [
            [[m_re[f, r0 + 8 * v:r0 + 8 * v + 8, :] for v in range(per)],
             [m_im[f, r0 + 8 * v:r0 + 8 * v + 8, :] for v in range(per)]]
            for f in range(nf)
        ]
        dsel = [[jnp.ones((8, nb), F32) for v in range(per)] for f in range(nf)]
        for v0 in range(per):
            c0 = r0 + 8 * v0
            B = [
                [[[lane_bcast(R[f][ri][v], c0 + c) for c in range(8)] for v in range(v0, per)] for ri in range(2)]
                for f in range(nf)
            ]
            for s in range(8):
                at_col = lane8 == c0 + s
                below = row8 > s
                for f in range(nf):
                    re, im = R[f]
                    b_re, b_im = B[f]
                    d = row_bcast(b_re[0][s], s)
                    ninv = -1.0 / d
                    dsel[f][v0] = jnp.where(row8 == s, d, dsel[f][v0])
                    p_re, p_im = row_bcast(re[v0], s), row_bcast(im[v0], s)
                    h_re = [row_bcast(b_re[0][c], s) if c > s else None for c in range(8)]
                    h_im = [row_bcast(b_im[0][c], s) if c > s else None for c in range(8)]
                    for v in range(v0, per):
                        i = v - v0
                        if i == 0 and s == 7:
                            continue
                        n_re = b_re[i][s] * ninv
                        n_im = b_im[i][s] * ninv
                        if i == 0:
                            n_re = jnp.where(below, n_re, 0.0)
                            n_im = jnp.where(below, n_im, 0.0)
                        for c in range(s + 1, 8):
                            b_re[i][c], b_im[i][c] = (
                                b_re[i][c] + (n_re * h_re[c] - n_im * h_im[c]),
                                b_im[i][c] + (n_re * h_im[c] + n_im * h_re[c]),
                            )
                        re[v], im[v] = (
                            jnp.where(at_col, n_re, re[v] + (n_re * p_re - n_im * p_im)),
                            jnp.where(at_col, n_im, im[v] + (n_re * p_im + n_im * p_re)),
                        )
        for f in range(nf):
            re, im = R[f]
            n_re, n_im = [], []
            for v in range(per):
                mine = row8 + (r0 + 8 * v)
                rs = lax.rsqrt(dsel[f][v])
                cut = (lane8 > mine) & (lane8 < r0 + block)
                n_re.append(jnp.where(cut, 0.0, jnp.where(lane8 == mine, rs, re[v] * rs)))
                n_im.append(jnp.where(cut | (lane8 == mine), 0.0, im[v] * rs))
            a_re = jnp.concatenate(n_re, axis=0)
            a_im = jnp.concatenate(n_im, axis=0)
            keep = lax.broadcasted_iota(jnp.int32, (block, nb), 1) < r0 + block
            w_ref[f, 0, r0:r0 + block, :] = jnp.where(keep, a_re, 0.0)
            w_ref[f, 1, r0:r0 + block, :] = jnp.where(keep, a_im, 0.0)
            if k + 1 < nb // block:
                rest = nb - r0 - block
                rh, rl = split2(a_re)
                ih, il = split2(a_im)
                lcat = jnp.concatenate([rh, ih, rh, ih, rl, il], axis=0)
                rcat = jnp.concatenate(
                    [jnp.concatenate([rh, ih, rl, il, rh, ih], axis=0),
                     jnp.concatenate([ih, -rh, il, -rl, ih, -rh], axis=0)], axis=1)
                upd = lax.dot_general(lcat, rcat, (((0,), (0,)), ((), ())), preferred_element_type=F32)
                upd = upd[r0 + block:, :]
                inside = lax.broadcasted_iota(jnp.int32, (rest, nb), 1)
                inside = (inside >= r0) & (inside < r0 + block)
                m_re[f, r0 + block:, :] = jnp.where(inside, 0.0, m_re[f, r0 + block:, :]) - upd[:, :nb]
                m_im[f, r0 + block:, :] = jnp.where(inside, 0.0, m_im[f, r0 + block:, :]) - upd[:, nb:]
    for f in range(nf):
        w_re, w_im = w_ref[f, 0], w_ref[f, 1]
        rh, rl = split2(w_re)
        ih, il = split2(w_im)
        x_re, x_im = q_ref[f, 0], q_ref[f, 1]
        x = jnp.concatenate([x_re, x_im], axis=0)
        a = jnp.concatenate([rh, -ih], axis=1)
        al = jnp.concatenate([rl, -il], axis=1)
        b = jnp.concatenate([ih, rh], axis=1)
        bl = jnp.concatenate([il, rl], axis=1)
        out_ref[f, 0] = jnp.dot(a, x, preferred_element_type=F32) + jnp.dot(al, x, preferred_element_type=F32)
        out_ref[f, 1] = jnp.dot(b, x, preferred_element_type=F32) + jnp.dot(bl, x, preferred_element_type=F32)


def finish(q, g, scale, block=16):
    nf, _, nb, cells = q.shape
    vm = pl.BlockSpec(memory_space=pltpu.VMEM)
    return pl.pallas_call(
        functools.partial(factor_kernel, scale, block),
        out_shape=jax.ShapeDtypeStruct((nf, 2, nb, cells), F32),
        in_specs=[vm, vm], out_specs=vm,
        scratch_shapes=[pltpu.VMEM((nf, nb, nb), F32), pltpu.VMEM((nf, nb, nb), F32), pltpu.VMEM((nf, 2, nb, nb), F32)],
        compiler_params=pltpu.CompilerParams(vmem_limit_bytes=32 << 20),
        name="factor_apply",
    )(q, g)


def local(snapshots, frequencies, offsets):
    total_cells = snapshots.shape[2] * lax.axis_size("space")
    q, g = exchange(snapshots, frequencies, offsets)
    return finish(q, g, 1.0 / total_cells)


def solution(mesh):
    placed = (P("tm", None, "space"), P(), P("tm"))
    return jax.shard_map(
        local, mesh=mesh, in_specs=placed, out_specs=P("tm", None, None, "space"), check_vma=False
    )
```

```python
import functools
import math

import jax
import jax.numpy as jnp
from jax import lax
from jax.experimental import pallas as pl
from jax.experimental.pallas import tpu as pltpu
from jax.sharding import PartitionSpec as P

F32 = jnp.float32
BF16 = jnp.bfloat16

MESH = pl.DeviceIdType.MESH
LANES = 128


def cos_sin(turns, length):
    quarter = length // 4
    shifted = turns + quarter // 2
    quadrant = lax.rem(lax.div(shifted, quarter), 4)
    theta = (lax.rem(shifted, quarter) - quarter // 2).astype(F32) * (2.0 * math.pi / length)
    sq = theta * theta
    cos_small = 1.0 + sq * (-0.5 + sq * (1 / 24 + sq * (-1 / 720 + sq * (1 / 40320 - sq / 3628800))))
    sin_small = theta * (1.0 + sq * (-1 / 6 + sq * (1 / 120 + sq * (-1 / 5040 + sq / 362880))))
    swap = (quadrant == 1) | (quadrant == 3)
    cos_sign = jnp.where((quadrant == 1) | (quadrant == 2), -1.0, 1.0)
    sin_sign = jnp.where(quadrant >= 2, -1.0, 1.0)
    return (
        jnp.where(swap, sin_small, cos_small) * cos_sign,
        jnp.where(swap, cos_small, sin_small) * sin_sign,
    )


def exchange_kernel(
    nt, nx, nl, nh, freq_hbm, off_hbm, snap_hbm, q_ref, g_ref,
    freq_ref, off_ref, snap, work, send, part, got, half_sum, got_far, final,
    far_ok, in_sem, a_send, a_recv, r_send, r_recv, f_send, f_recv, w_send, w_recv, own_sem,
):
    nf_all = freq_ref.shape[0]
    blocks, length, cells = snap.shape
    nf = nf_all // nt
    nb = blocks * nt
    halves = cells // LANES
    group = nx * nl
    me = lax.axis_index("tm")
    spot = lax.axis_index("space")
    my_far = lax.div(spot, group)
    my_near = lax.rem(spot, group)
    my_l = lax.div(my_near, nx)
    my_x = lax.rem(my_near, nx)
    my_y = lax.div(me, 2)
    core = lax.rem(me, 2)
    owns = core * lax.div(lax.rem(my_l + 1, nl), 2)
    flip = lax.div(my_far, 2)
    my_m = (my_l - 1) + flip * (3 - 2 * my_l)

    def tm_peer(d):
        return (lax.rem(me + d, nt), spot)

    def plane(far, m):
        return 1 + m + lax.div(far, 2) * (1 - 2 * m)

    def owner(m, dx):
        return (2 * my_y + 1, my_far * group + plane(my_far, m) * nx + lax.rem(my_x + dx, nx))

    def not_me(m, dx):
        return (core == 0) | (my_l != plane(my_far, m)) if dx == 0 else my_x >= 0

    def client(c, dl, dx):
        return (2 * my_y + c, my_far * group + lax.rem(my_l + dl, nl) * nx + lax.rem(my_x + dx, nx))

    def far_owner(d):
        far = lax.rem(my_far + d, nh)
        return (me, far * group + plane(far, my_m) * nx + my_x)

    def rank(far):
        return far + lax.div(far, 2) * (5 - 2 * far)

    my_rank = rank(my_far)

    def far_rank(d):
        return rank(lax.rem(my_far + d, nh))

    order = (2, 1, 3, 0)
    targets = [(m, dx) for dx in order for m in range(2)]
    clients = [(c, dl, dx) for c in (1, 0) for dx in order for dl in order if dl or dx or c == 0]

    barrier = pltpu.get_barrier_semaphore()

    @pl.when(owns == 1)
    def _():
        for d in range(1, nh):
            @pl.when(far_rank(d) > my_rank)
            def _():
                pl.semaphore_signal(barrier, inc=1, device_id=far_owner(d), device_id_type=MESH)
        for c, dl, dx in clients:
            pl.semaphore_signal(barrier, inc=1, device_id=client(c, dl, dx), device_id_type=MESH)

    for m, dx in targets:
        @pl.when(not_me(m, dx))
        def _():
            pl.semaphore_signal(barrier, inc=1, device_id=owner(m, dx), device_id_type=MESH)

    for d in range(1, nt):
        pl.semaphore_signal(barrier, inc=1, device_id=tm_peer(d), device_id_type=MESH)

    small = [
        pltpu.make_async_copy(freq_hbm, freq_ref, in_sem.at[4]),
        pltpu.make_async_copy(off_hbm, off_ref, in_sem.at[5]),
    ]
    for load in small:
        load.start()
    step = blocks // 4
    loads = [
        pltpu.make_async_copy(snap_hbm.at[pl.ds(i * step, step)], snap.at[pl.ds(i * step, step)], in_sem.at[i])
        for i in range(4)
    ]
    for load in loads:
        load.start()

    row = lax.broadcasted_iota(jnp.int32, (nf_all, length), 0)
    position = lax.broadcasted_iota(jnp.int32, (nf_all, length), 1)
    for load in small:
        load.wait()
    freq = jnp.zeros((nf_all, length), jnp.int32)
    start = jnp.zeros((nf_all, length), jnp.int32)
    for j in range(nf_all):
        freq = jnp.where(row == j, freq_ref[j], freq)
    for b in range(blocks):
        start = jnp.where(position == b, off_ref[b], start)
    window = 0.5 - 0.5 * cos_sin(position, length)[0]
    cosine, sine = cos_sin(lax.rem(freq * position, length), length)
    table = jnp.concatenate([window * cosine, window * sine], axis=0).astype(BF16)
    cos_phase, sin_phase = cos_sin(lax.rem(freq * lax.rem(start, length), length), length)

    for b in range(blocks):
        if b % step == 0:
            loads[b // step].wait()
        both = jnp.dot(table, snap[b], preferred_element_type=F32)
        cos_part, sin_part = both[:nf_all], both[nf_all:]
        cp, sp = cos_phase[:, b:b + 1], sin_phase[:, b:b + 1]
        base = b * 2 * nf_all
        real = cos_part * cp - sin_part * sp
        imag = -(sin_part * cp + cos_part * sp)
        for h in range(halves):
            work[h, base:base + nf_all, :] = real[:, h * LANES:(h + 1) * LANES]
            work[h, base + nf_all:base + 2 * nf_all, :] = imag[:, h * LANES:(h + 1) * LANES]

    mine = pl.ds(pl.multiple_of(me * blocks, blocks), blocks)

    def a_copy(f, d):
        return pltpu.make_async_remote_copy(
            src_ref=send.at[f, lax.rem(me + d, nt)],
            dst_ref=q_ref.at[f, :, mine, :],
            send_sem=a_send.at[f, d], recv_sem=a_recv.at[f, d],
            device_id=tm_peer(d), device_id_type=MESH)

    own = [pltpu.make_async_copy(send.at[f, me], q_ref.at[f, :, mine, :], own_sem.at[f]) for f in range(nf)]
    for f in range(nf):
        for t in range(nt):
            for ri in range(2):
                for h in range(halves):
                    rows = work[h, pl.ds(ri * nf_all + t * nf + f, blocks, stride=2 * nf_all), :]
                    send[f, t, ri, :, h * LANES:(h + 1) * LANES] = rows.astype(BF16)
        if f == 0:
            pl.semaphore_wait(barrier, nt - 1 + 2 * nx + owns * (len(clients) - 1 + my_rank))
        for d in (4, 3, 5, 2, 6, 1, 7):
            a_copy(f, d).start()
        own[f].start()

    @pl.when(owns == 1)
    def _():
        for d in range(1, nh):
            @pl.when(far_rank(d) < my_rank)
            def _():
                pl.semaphore_signal(far_ok.at[nh - d], inc=1, device_id=far_owner(d), device_id_type=MESH)

    grow = lax.broadcasted_iota(jnp.int32, (nb, nb), 0)
    glane = lax.broadcasted_iota(jnp.int32, (nb, nb), 1)
    wide = nb // (2 * nx)

    def chunk(m, x):
        return pl.ds(pl.multiple_of((m * nx + x) * wide, wide), wide)

    for f in range(nf):
        own[f].wait()
        for d in range(1, nt):
            a_copy(f, d).wait_recv()
        rows = q_ref[f].reshape(2 * nb, cells)
        full = lax.dot_general(rows, rows, (((1,), (1,)), ((), ())), preferred_element_type=F32)
        real = full[:nb, :nb] + full[nb:, nb:]
        imag = full[nb:, :nb] - full[:nb, nb:]
        part[f] = jnp.where(grow >= glane, real, imag)

    def r_copy(m, dx):
        spot_there = lax.rem(my_l - plane(my_far, m) + nl, nl) * nx + (nx - dx) % nx
        return pltpu.make_async_remote_copy(
            src_ref=part.at[:, chunk(m, lax.rem(my_x + dx, nx)), :], dst_ref=got.at[core, spot_there],
            send_sem=r_send.at[m, dx], recv_sem=r_recv.at[core, spot_there],
            device_id=owner(m, dx), device_id_type=MESH)

    for m, dx in targets:
        @pl.when(not_me(m, dx))
        def _():
            r_copy(m, dx).start()

    my_chunk = chunk(my_m, my_x)

    def r_arrival(c, i):
        return pltpu.make_async_remote_copy(
            src_ref=half_sum.at[0], dst_ref=got.at[c, i], send_sem=r_send.at[0, 0], recv_sem=r_recv.at[c, i],
            device_id=tm_peer(1), device_id_type=MESH)

    def f_copy(c, d):
        return pltpu.make_async_remote_copy(
            src_ref=half_sum.at[c], dst_ref=got_far.at[my_far, c],
            send_sem=f_send.at[c, d], recv_sem=f_recv.at[c, d],
            device_id=far_owner(d), device_id_type=MESH)

    def w_copy(c, dl, dx):
        return pltpu.make_async_remote_copy(
            src_ref=final.at[c], dst_ref=g_ref.at[:, my_chunk, :],
            send_sem=w_send.at[c, dl * nx + dx], recv_sem=w_recv.at[my_m * nx + my_x],
            device_id=client(c, dl, dx), device_id_type=MESH)

    @pl.when(owns == 1)
    def _():
        for c in (1, 0):
            total = part[:, my_chunk, :] if c == 1 else None
            for i in range(group):
                if c == 0 or i > 0:
                    r_arrival(c, i).wait_recv()
                    total = got[c, i] if total is None else total + got[c, i]
            half_sum[c] = total
            got_far[my_far, c] = total
            for d in (2, 1, 3):
                @pl.when(far_rank(d) < my_rank)
                def _():
                    f_copy(c, d).start()
            for d in (1, 3, 2):
                @pl.when(far_rank(d) > my_rank)
                def _():
                    if c == 1:
                        pl.semaphore_wait(far_ok.at[d], 1)
                    f_copy(c, d).start()
        for c in (1, 0):
            for d in (1, 3, 2):
                f_copy(c, d).wait_recv()
            total = got_far[0, c]
            for i in range(1, nh):
                total = total + got_far[i, c]
            final[c] = total
            for cc, dl, dx in clients:
                if cc == c:
                    w_copy(cc, dl, dx).start()
        g_ref[:, my_chunk, :] = final[1]

    def w_arrival(slot):
        return pltpu.make_async_remote_copy(
            src_ref=final.at[0], dst_ref=g_ref.at[:, pl.ds(slot * wide, wide), :],
            send_sem=w_send.at[0, 0], recv_sem=w_recv.at[slot],
            device_id=tm_peer(1), device_id_type=MESH)

    for slot in range(2 * nx):
        @pl.when((owns == 0) | (my_m * nx + my_x != slot))
        def _():
            w_arrival(slot).wait_recv()

    for f in range(nf):
        for d in range(1, nt):
            a_copy(f, d).wait_send()
    for m, dx in targets:
        @pl.when(not_me(m, dx))
        def _():
            r_copy(m, dx).wait_send()

    @pl.when(owns == 1)
    def _():
        for c in range(2):
            for d in range(1, nh):
                f_copy(c, d).wait_send()
        for c, dl, dx in clients:
            w_copy(c, dl, dx).wait_send()


def exchange(snapshots, frequencies, offsets):
    nt = lax.axis_size("tm")
    nx, nl = 4, 4
    group = nx * nl
    nh = lax.axis_size("space") // group
    blocks, length, cells = snapshots.shape
    nf_all = frequencies.shape[0]
    nf, nb = nf_all // nt, blocks * nt
    wide = nb // (2 * nx)
    halves = cells // LANES
    vm = pl.BlockSpec(memory_space=pltpu.VMEM)
    dma = pltpu.SemaphoreType.DMA
    q, g = pl.pallas_call(
        functools.partial(exchange_kernel, nt, nx, nl, nh),
        out_shape=(jax.ShapeDtypeStruct((nf, 2, nb, cells), BF16), jax.ShapeDtypeStruct((nf, nb, nb), F32)),
        in_specs=[pl.BlockSpec(memory_space=pltpu.HBM)] * 3, out_specs=(vm, vm),
        scratch_shapes=[
            pltpu.SMEM((nf_all,), jnp.int32),
            pltpu.SMEM((blocks,), jnp.int32),
            pltpu.VMEM((blocks, length, cells), BF16),
            pltpu.VMEM((halves, blocks * 2 * nf_all, LANES), F32),
            pltpu.VMEM((nf, nt, 2, blocks, cells), BF16),
            pltpu.VMEM((nf, nb, nb), F32),
            pltpu.VMEM((2, group, nf, wide, nb), F32),
            pltpu.VMEM((2, nf, wide, nb), F32),
            pltpu.VMEM((nh, 2, nf, wide, nb), F32),
            pltpu.VMEM((2, nf, wide, nb), F32),
            pltpu.SemaphoreType.REGULAR((nh,)), dma((6,)), dma((nf, nt)), dma((nf, nt)), dma((2, nx)), dma((2, group)),
            dma((2, nh)), dma((2, nh)), dma((2, group)), dma((2 * nx,)), dma((nf,)),
        ],
        compiler_params=pltpu.CompilerParams(
            collective_id=0, has_side_effects=True, vmem_limit_bytes=53 << 20),
        name="exchange_gram",
    )(*[pltpu.with_memory_space_constraint(a, pltpu.HBM) for a in (frequencies, offsets, snapshots)])
    return q, g


def split2(v):
    hi = v.astype(BF16)
    lo = (v - hi.astype(F32)).astype(BF16)
    return hi, lo


def lane_bcast(v, col):
    return jnp.broadcast_to(v[:, col:col + 1], v.shape)


def row_bcast(v, s):
    return jnp.broadcast_to(v[s:s + 1, :], v.shape)


def factor_kernel(scale, block, q_ref, g_ref, out_ref, m_re, m_im, w_ref):
    nf, _, nb, cells = q_ref.shape
    row8 = lax.broadcasted_iota(jnp.int32, (8, nb), 0)
    lane8 = lax.broadcasted_iota(jnp.int32, (8, nb), 1)
    row = lax.broadcasted_iota(jnp.int32, (nb, nb), 0)
    lane = lax.broadcasted_iota(jnp.int32, (nb, nb), 1)
    for f in range(nf):
        packed = g_ref[f] * scale
        flipped = packed.T
        m_re[f] = jnp.where(row >= lane, packed, flipped)
        m_im[f] = jnp.where(row > lane, -flipped, jnp.where(row < lane, packed, 0.0))
    per = block // 8
    for k in range(nb // block):
        r0 = k * block
        R = [
            [[m_re[f, r0 + 8 * v:r0 + 8 * v + 8, :] for v in range(per)],
             [m_im[f, r0 + 8 * v:r0 + 8 * v + 8, :] for v in range(per)]]
            for f in range(nf)
        ]
        dsel = [[jnp.ones((8, nb), F32) for v in range(per)] for f in range(nf)]
        for v0 in range(per):
            c0 = r0 + 8 * v0
            B = [
                [[[lane_bcast(R[f][ri][v], c0 + c) for c in range(8)] for v in range(v0, per)] for ri in range(2)]
                for f in range(nf)
            ]
            for s in range(8):
                at_col = lane8 == c0 + s
                below = row8 > s
                for f in range(nf):
                    re, im = R[f]
                    b_re, b_im = B[f]
                    d = row_bcast(b_re[0][s], s)
                    ninv = -1.0 / d
                    dsel[f][v0] = jnp.where(row8 == s, d, dsel[f][v0])
                    p_re, p_im = row_bcast(re[v0], s), row_bcast(im[v0], s)
                    h_re = [row_bcast(b_re[0][c], s) if c > s else None for c in range(8)]
                    h_im = [row_bcast(b_im[0][c], s) if c > s else None for c in range(8)]
                    for v in range(v0, per):
                        i = v - v0
                        if i == 0 and s == 7:
                            continue
                        n_re = b_re[i][s] * ninv
                        n_im = b_im[i][s] * ninv
                        if i == 0:
                            n_re = jnp.where(below, n_re, 0.0)
                            n_im = jnp.where(below, n_im, 0.0)
                        for c in range(s + 1, 8):
                            b_re[i][c], b_im[i][c] = (
                                b_re[i][c] + (n_re * h_re[c] - n_im * h_im[c]),
                                b_im[i][c] + (n_re * h_im[c] + n_im * h_re[c]),
                            )
                        re[v], im[v] = (
                            jnp.where(at_col, n_re, re[v] + (n_re * p_re - n_im * p_im)),
                            jnp.where(at_col, n_im, im[v] + (n_re * p_im + n_im * p_re)),
                        )
        for f in range(nf):
            re, im = R[f]
            n_re, n_im = [], []
            for v in range(per):
                mine = row8 + (r0 + 8 * v)
                rs = lax.rsqrt(dsel[f][v])
                cut = (lane8 > mine) & (lane8 < r0 + block)
                n_re.append(jnp.where(cut, 0.0, jnp.where(lane8 == mine, rs, re[v] * rs)))
                n_im.append(jnp.where(cut | (lane8 == mine), 0.0, im[v] * rs))
            a_re = jnp.concatenate(n_re, axis=0)
            a_im = jnp.concatenate(n_im, axis=0)
            keep = lax.broadcasted_iota(jnp.int32, (block, nb), 1) < r0 + block
            w_ref[f, 0, r0:r0 + block, :] = jnp.where(keep, a_re, 0.0)
            w_ref[f, 1, r0:r0 + block, :] = jnp.where(keep, a_im, 0.0)
            if k + 1 < nb // block:
                rest = nb - r0 - block
                rh, rl = split2(a_re)
                ih, il = split2(a_im)
                lcat = jnp.concatenate([rh, ih, rh, ih, rl, il], axis=0)
                rcat = jnp.concatenate(
                    [jnp.concatenate([rh, ih, rl, il, rh, ih], axis=0),
                     jnp.concatenate([ih, -rh, il, -rl, ih, -rh], axis=0)], axis=1)
                upd = lax.dot_general(lcat, rcat, (((0,), (0,)), ((), ())), preferred_element_type=F32)
                upd = upd[r0 + block:, :]
                inside = lax.broadcasted_iota(jnp.int32, (rest, nb), 1)
                inside = (inside >= r0) & (inside < r0 + block)
                m_re[f, r0 + block:, :] = jnp.where(inside, 0.0, m_re[f, r0 + block:, :]) - upd[:, :nb]
                m_im[f, r0 + block:, :] = jnp.where(inside, 0.0, m_im[f, r0 + block:, :]) - upd[:, nb:]
    for f in range(nf):
        w_re, w_im = w_ref[f, 0], w_ref[f, 1]
        rh, rl = split2(w_re)
        ih, il = split2(w_im)
        x_re, x_im = q_ref[f, 0], q_ref[f, 1]
        x = jnp.concatenate([x_re, x_im], axis=0)
        a = jnp.concatenate([rh, -ih], axis=1)
        al = jnp.concatenate([rl, -il], axis=1)
        b = jnp.concatenate([ih, rh], axis=1)
        bl = jnp.concatenate([il, rl], axis=1)
        out_ref[f, 0] = jnp.dot(a, x, preferred_element_type=F32) + jnp.dot(al, x, preferred_element_type=F32)
        out_ref[f, 1] = jnp.dot(b, x, preferred_element_type=F32) + jnp.dot(bl, x, preferred_element_type=F32)


def finish(q, g, scale, block=16):
    nf, _, nb, cells = q.shape
    vm = pl.BlockSpec(memory_space=pltpu.VMEM)
    return pl.pallas_call(
        functools.partial(factor_kernel, scale, block),
        out_shape=jax.ShapeDtypeStruct((nf, 2, nb, cells), F32),
        in_specs=[vm, vm], out_specs=vm,
        scratch_shapes=[pltpu.VMEM((nf, nb, nb), F32), pltpu.VMEM((nf, nb, nb), F32), pltpu.VMEM((nf, 2, nb, nb), F32)],
        compiler_params=pltpu.CompilerParams(vmem_limit_bytes=32 << 20),
        name="factor_apply",
    )(q, g)


def local(snapshots, frequencies, offsets):
    total_cells = snapshots.shape[2] * lax.axis_size("space")
    q, g = exchange(snapshots, frequencies, offsets)
    return finish(q, g, 1.0 / total_cells)


def solution(mesh):
    placed = (P("tm", None, "space"), P(), P("tm"))
    return jax.shard_map(
        local, mesh=mesh, in_specs=placed, out_specs=P("tm", None, None, "space"), check_vma=False
    )
```
